32 devices in a mesh: dp: 8 (over z, x), row: 4 (over y, core).
Axes of the slice: x: 2, y: 2, z: 4, core: 2. Of those that a mesh axis runs over, the one named last changes fastest.
Arguments:
- queries: bfloat16 [2048, 4096], P('dp', 'row'), may hold values from -100 to 100
- passages: bfloat16 [2048, 4096], P('dp', 'row'), may hold values from -10 to 10
- cached: bfloat16 [16384, 4096], P('dp', 'row'), may hold values from -6 to 6
- hard_shard: int32 [2048, 4], P('dp'), may hold values from 0 to 7, as said below
- hard_row: int32 [2048, 4], P('dp'), may hold values from 0 to 2047
- query_source: int32 [2048], P('dp'), may hold values from 0 to 7
- block_source: int32 [16], replicated, may hold values from 0 to 7
Outputs:
- mean_loss: float32 [], replicated
- query_grad: bfloat16 [2048, 4096], P('dp', 'row')
- passage_grad: bfloat16 [2048, 4096], P('dp', 'row')
The draws below stay inside these ranges and needn't reach their ends.
Inputs may be any that keep to these rules, and one draw needn't show every extreme that they name: `hard_shard`: one cache shard, drawn with the seed, is named exactly 256 times among the 256 queries of every device; among one device's queries no shard is named more than 256 times, and the other shards share the rest as evenly as possible; a query's 4 hard negatives lie in 4 different shards.
All inputs are finite; a program needn't handle non-finite values.
Results may differ from the reference program's by a relative error of at most 0.0043.
Values may be sent and summed in bfloat16 or wider, within the bound.
A program may use at most 128 MiB of HBM per device.

```python
import math
import jax
import jax.numpy as jnp
from jax import lax

D = 4096
ROWS = 256
CD = 2048
H = 4
BLOCK = 128
NSRC = 8
NQ = 2048
NP = 2048
NC = 16384
NB = 16


def cache_rows(key, indices):
    cache_key = jax.random.fold_in(key, 31)

    def one_row(index):
        row_key = jax.random.fold_in(cache_key, index)
        return jnp.clip(jax.random.normal(row_key, (D,), jnp.float32), -6.0, 6.0)
    return jax.vmap(one_row)(indices)


def hard_indices(key):
    index_key = jax.random.fold_in(key, 47)
    hot_key, order_key, row_key = jax.random.split(index_key, 3)
    n_data = NQ // ROWS
    capacity = min(ROWS, 3 * ROWS * H // n_data)
    hottest = jax.random.randint(hot_key, (), 0, n_data, dtype=jnp.int32)
    hard_slots = jnp.arange(H, dtype=jnp.int32)

    def one_block(block_key):
        first_key, second_key = jax.random.split(block_key)
        placed = jax.random.permutation(first_key, ROWS).astype(jnp.int32)[:, None]
        others = jax.random.permutation(second_key, n_data - 1).astype(jnp.int32)
        early = placed < capacity
        counter = placed * H + hard_slots[None, :] - jnp.minimum(placed, capacity) - early.astype(jnp.int32)
        counter = jnp.maximum(counter, 0)
        other_shard = (hottest + 1 + others[counter % (n_data - 1)]) % n_data
        is_hot = early & (hard_slots[None, :] == 0)
        return jnp.where(is_hot, hottest, other_shard).astype(jnp.int32)
    block_keys = jax.random.split(order_key, n_data)
    shard_ids = jax.vmap(one_block)(block_keys).reshape(NQ, H)
    row_ids = jax.random.randint(row_key, (NQ, H), 0, CD, dtype=jnp.int32)
    return (shard_ids, row_ids)


def passage_base(key):
    own_key, topic_key, share_key = jax.random.split(jax.random.fold_in(key, 11), 3)
    topic_count = NP // 16
    own_part = jnp.clip(jax.random.normal(own_key, (NP, D), jnp.float32), -6.0, 6.0)
    topic_part = jnp.clip(jax.random.normal(topic_key, (topic_count, D), jnp.float32), -6.0, 6.0)
    shares = jax.random.uniform(share_key, (topic_count, 1), jnp.float32, 0.3, 0.8)
    members = jnp.tile(topic_part, (16, 1))
    member_share = jnp.tile(shares, (16, 1))
    values = jnp.sqrt(1.0 - member_share) * own_part + jnp.sqrt(member_share) * members
    return values


def draw_passages(key, part):
    return passage_base(key).astype(jnp.bfloat16)


def draw_cached(key, part):
    return cache_rows(key, jnp.arange(NC, dtype=jnp.int32)).astype(jnp.bfloat16)


def draw_hard_shard(key, part):
    return hard_indices(key)[0]


def draw_hard_row(key, part):
    return hard_indices(key)[1]


def draw_queries(key, part):
    own_key, match_key, pull_key = jax.random.split(jax.random.fold_in(key, 23), 3)
    passage_values = passage_base(key)
    shard_ids, row_ids = hard_indices(key)
    root_width = math.sqrt(D)
    match_scale = jnp.exp(jax.random.uniform(match_key, (NQ, 1), jnp.float32, math.log(5.0), math.log(14.0))) / root_width
    pull_scale = jnp.exp(jax.random.uniform(pull_key, (NQ, H), jnp.float32, math.log(4.0), math.log(13.0))) / root_width
    values = jnp.clip(jax.random.normal(own_key, (NQ, D), jnp.float32), -6.0, 6.0) + match_scale * passage_values
    for hard_slot in range(H):
        flat_index = (shard_ids[:, hard_slot] * CD + row_ids[:, hard_slot]).astype(jnp.int32)
        values = values + pull_scale[:, hard_slot:hard_slot + 1] * cache_rows(key, flat_index)
    return values.astype(jnp.bfloat16)


def place_ends(array, rng, low, largest):
    index_at = [jax.random.randint(jax.random.fold_in(rng, axis), (), 0, length) for axis, length in enumerate(array.shape)]
    widest = array.shape.index(max(array.shape))
    next_to = index_at[:widest] + [(index_at[widest] + 1) % array.shape[widest]] + index_at[widest + 1:]
    return array.at[tuple(index_at)].set(low).at[tuple(next_to)].set(largest)


def setup_inputs(seed: int = 0) -> dict:
    splits = jax.random.split(jax.random.key(seed), 8)
    return {
        "queries": draw_queries(jax.random.fold_in(splits[7], 71), 0),
        "passages": draw_passages(jax.random.fold_in(splits[7], 71), 0),
        "cached": draw_cached(jax.random.fold_in(splits[7], 71), 0),
        "hard_shard": draw_hard_shard(jax.random.fold_in(splits[7], 71), 0),
        "hard_row": draw_hard_row(jax.random.fold_in(splits[7], 71), 0),
        "query_source": place_ends(jax.random.randint(splits[5], (NQ,), 0, NSRC), jax.random.fold_in(splits[5], 1), 0, NSRC - 1).astype(jnp.int32),
        "block_source": place_ends(jax.random.randint(splits[6], (NB,), 0, NSRC), jax.random.fold_in(splits[6], 1), 0, NSRC - 1).astype(jnp.int32),
    }


NEG_FILL = -1e+30

def reference(queries, passages, cached, hard_shard, hard_row, query_source, block_source):
    logit_scale = 1.0 / math.sqrt(D)
    logits = logit_scale * jnp.dot(queries, passages.T, preferred_element_type=jnp.float32)
    cache_index = (hard_shard * CD + hard_row).astype(jnp.int32)
    hard_rows = jnp.take(cached, cache_index.reshape(-1), axis=0).reshape(NQ, H, D)
    hard_logits = logit_scale * jnp.einsum('qd,qhd->qh', queries.astype(jnp.float32), hard_rows.astype(jnp.float32))
    columns = jnp.arange(NP, dtype=jnp.int32)
    targets = jnp.arange(NQ, dtype=jnp.int32)
    column_source = jnp.repeat(block_source, BLOCK)
    positive = columns[None, :] == targets[:, None]
    allowed = (query_source[:, None] != column_source[None, :]) | positive
    masked = jnp.where(allowed, logits, NEG_FILL)
    maximum = jnp.maximum(lax.optimization_barrier(jnp.max(masked, axis=1)), lax.optimization_barrier(jnp.max(hard_logits, axis=1)))
    exponent = jnp.exp(masked - maximum[:, None])
    hard_expo = jnp.exp(hard_logits - maximum[:, None])
    totals = lax.optimization_barrier(jnp.sum(exponent, axis=1)) + lax.optimization_barrier(jnp.sum(hard_expo, axis=1))
    pos_logit = lax.optimization_barrier(jnp.sum(jnp.where(positive, logits, 0.0), axis=1))
    per_query = maximum + jnp.log(totals) - pos_logit
    mean_loss = jnp.sum(per_query) / NQ
    weights = (exponent / totals[:, None] - positive.astype(jnp.float32)).astype(jnp.bfloat16)
    hard_weights = (hard_expo / totals[:, None]).astype(jnp.bfloat16)
    query_grad = jnp.dot(weights, passages, preferred_element_type=jnp.float32)
    query_grad = query_grad + jnp.einsum('qh,qhd->qd', hard_weights.astype(jnp.float32), hard_rows.astype(jnp.float32))
    passage_grad = jnp.dot(weights.T, queries, preferred_element_type=jnp.float32)
    return (mean_loss, query_grad.astype(jnp.bfloat16), passage_grad.astype(jnp.bfloat16))
```

```python
import functools
import math

import jax
import jax.numpy as jnp
from jax import lax
from jax.experimental import pallas as pl
from jax.experimental.pallas import tpu as pltpu
from jax.sharding import PartitionSpec as P

D = 4096
BLOCK = 128
LANES = 128
NEG_FILL = -1e30
MESH = pl.DeviceIdType.MESH


def spill_kernel(n, hot, rows_ref, out, send, recv, own_sem):
    me = lax.axis_index("dp")
    r = lax.axis_index("row")
    barrier = pltpu.get_barrier_semaphore()

    def copy(j):
        to = (hot + j) % n
        return pltpu.make_async_remote_copy(
            src_ref=rows_ref.at[to],
            dst_ref=out,
            send_sem=send.at[j - 1],
            recv_sem=recv,
            device_id=(to, r),
            device_id_type=MESH,
        )

    @pl.when(me == hot)
    def _():
        for j in range(1, n):
            pl.semaphore_signal(
                barrier, inc=1, device_id=((hot + j) % n, r), device_id_type=MESH
            )

    @pl.when(me != hot)
    def _():
        pl.semaphore_signal(barrier, inc=1, device_id=(hot, r), device_id_type=MESH)

    pl.semaphore_wait(barrier, 1 + (me == hot).astype(jnp.int32) * (n - 2))

    @pl.when(me == hot)
    def _():
        for j in range(1, n):
            copy(j).start()
        own = pltpu.make_async_copy(rows_ref.at[hot], out, own_sem)
        own.start()
        own.wait()
        for j in range(1, n):
            copy(j).wait_send()

    @pl.when(me != hot)
    def _():
        copy(1).wait_recv()


def spill(n, hot, rows):
    vmem = pl.BlockSpec(memory_space=pltpu.VMEM)
    dma = pltpu.SemaphoreType.DMA
    return pl.pallas_call(
        functools.partial(spill_kernel, n, hot),
        name=f"spill_{hot}",
        out_shape=jax.ShapeDtypeStruct(rows.shape[1:], rows.dtype),
        in_specs=[vmem],
        out_specs=vmem,
        scratch_shapes=[dma((n - 1,)), dma(()), dma(())],
        compiler_params=pltpu.CompilerParams(collective_id=3 + hot, has_side_effects=True),
    )(rows)


def fetch_hard(cached, hard_shard, hard_row, n_data):
    row_count, hard_count = hard_shard.shape
    width_dev = cached.shape[1]
    capacity = min(row_count, 3 * row_count * hard_count // n_data)
    others = -(-(row_count * hard_count - capacity) // (n_data - 1))
    common = min(capacity - 16, -(-others // 16) * 16)
    owners = hard_shard.reshape(-1)
    wanted = hard_row.reshape(-1)
    one_hot = (owners[:, None] == jnp.arange(n_data, dtype=jnp.int32)[None, :]).astype(jnp.int32)
    before = jnp.cumsum(one_hot, axis=0) - one_hot
    slot_index = jnp.sum(before * one_hot, axis=1)
    hot = jnp.argmax(jnp.sum(one_hot, axis=0)).astype(jnp.int32)
    target = owners * capacity + slot_index
    requests = (
        jnp.zeros((n_data * capacity,), jnp.int32).at[target].set(wanted).reshape(n_data, capacity)
    )
    asked_rows = lax.all_to_all(requests, "dp", split_axis=0, concat_axis=0, tiled=True)
    picked = jnp.take(cached, asked_rows[:, :common].reshape(-1), axis=0, mode="clip")
    picked = picked.reshape(n_data, common, width_dev)
    replies = lax.all_to_all(picked, "dp", split_axis=0, concat_axis=0, tiled=True)
    extra = jnp.take(cached, asked_rows[:, common:].reshape(-1), axis=0, mode="clip")
    extra = extra.reshape(n_data, capacity - common, width_dev)
    spilled = lax.switch(hot, [functools.partial(spill, n_data, k) for k in range(n_data)], extra)
    reply_rows = jnp.concatenate([replies.reshape(n_data * common, width_dev), spilled], axis=0)
    place = jnp.where(
        slot_index < common, owners * common + slot_index, n_data * common + slot_index - common
    )
    by_slot = place.reshape(row_count, hard_count).T.reshape(-1)
    hard_rows = jnp.take(reply_rows, by_slot, axis=0, mode="clip")
    return hard_rows.reshape(hard_count, row_count, width_dev)


def gather_kernel(n, n_row, q_ref, p_ref, pall, qall, lsum, lpart, lrecv,
                  gsend, grecv, lsend, lrecv_sem, own_sem):
    me = lax.axis_index("dp")
    r = lax.axis_index("row")
    lines = n // 2
    a = me // 2
    b = me % 2
    rows = q_ref.shape[0]
    part = rows // n_row
    across = a * 2 + 1 - b

    barrier = pltpu.get_barrier_semaphore()
    pl.semaphore_signal(barrier, inc=1, device_id=(across, r), device_id_type=MESH)
    for k in range(1, n_row):
        pl.semaphore_signal(
            barrier, inc=1, device_id=(me, lax.rem(r + k, n_row)), device_id_type=MESH
        )

    @pl.when(a < lines - 1)
    def _():
        pl.semaphore_signal(barrier, inc=1, device_id=(me + 2, r), device_id_type=MESH)

    @pl.when(a > 0)
    def _():
        pl.semaphore_signal(barrier, inc=1, device_id=(me - 2, r), device_id_type=MESH)

    neighbours = (a < lines - 1).astype(jnp.int32) + (a > 0).astype(jnp.int32)
    pl.semaphore_wait(barrier, n_row + neighbours)

    alls = (pall, qall)
    own = (p_ref, q_ref)

    def copy(t, kind, blk, first=False):
        to = (across, me + 2, me - 2)[kind]
        return pltpu.make_async_remote_copy(
            src_ref=own[t] if first else alls[t].at[blk],
            dst_ref=alls[t].at[blk],
            send_sem=gsend.at[t, kind, blk],
            recv_sem=grecv.at[t, blk],
            device_id=(to, r),
            device_id_type=MESH,
        )

    def arrived(t, blk):
        copy(t, 0, blk).wait_recv()

    def start_own(t):
        @pl.when(a < lines - 1)
        def _():
            copy(t, 1, me, True).start()

        @pl.when(a > 0)
        def _():
            copy(t, 2, me, True).start()

        copy(t, 0, me, True).start()

    def multiply(blk, block):
        lpart[blk] = lax.dot_general(
            q_ref[...], block, (((1,), (1,)), ((), ())), preferred_element_type=jnp.float32
        )

    def ship(blk):
        for k in range(1, n_row):
            to = lax.rem(r + k, n_row)
            ship_copy(blk, to, k).start()

    def ship_copy(blk, to, k):
        return pltpu.make_async_remote_copy(
            src_ref=lpart.at[blk, pl.ds(pl.multiple_of(to * part, part), part), :],
            dst_ref=lrecv.at[k - 1, blk],
            send_sem=lsend.at[k - 1, blk],
            recv_sem=lrecv_sem.at[k - 1, blk],
            device_id=(me, to),
            device_id_type=MESH,
        )

    def relay(t, s):
        lo = me - 2 * (s + 1)
        hi = me + 2 * (s + 1)

        @pl.when(lo >= 0)
        def _():
            arrived(t, lo)

            @pl.when(a < lines - 1)
            def _():
                copy(t, 1, lo).start()

            copy(t, 0, lo).start()

        @pl.when(hi < n)
        def _():
            arrived(t, hi)

            @pl.when(a > 0)
            def _():
                copy(t, 2, hi).start()

            copy(t, 0, hi).start()

    def logits_of(s):
        lo = me - 2 * (s + 1)
        hi = me + 2 * (s + 1)
        flip = 1 - 2 * b

        @pl.when(lo >= 0)
        def _():
            multiply(lo, pall[lo])

        @pl.when(hi < n)
        def _():
            multiply(hi, pall[hi])

        @pl.when(lo >= 0)
        def _():
            ship(lo)
            arrived(0, lo + flip)
            multiply(lo + flip, pall[lo + flip])

        @pl.when(hi < n)
        def _():
            ship(hi)
            arrived(0, hi + flip)
            multiply(hi + flip, pall[hi + flip])

        @pl.when(lo >= 0)
        def _():
            ship(lo + flip)

        @pl.when(hi < n)
        def _():
            ship(hi + flip)

    start_own(0)
    own_p = pltpu.make_async_copy(p_ref, pall.at[me], own_sem.at[0])
    own_q = pltpu.make_async_copy(q_ref, qall.at[me], own_sem.at[1])
    own_p.start()
    own_q.start()
    multiply(me, p_ref[...])
    for s in range(lines - 1):
        relay(0, s)
        if s == lines - 2:
            start_own(1)
        if s == 0:
            ship(me)
            arrived(0, across)
            multiply(across, pall[across])
            ship(across)
        else:
            logits_of(s - 1)
    for s in range(lines - 1):
        relay(1, s)
        if s == 0:
            logits_of(lines - 2)
    arrived(1, across)
    flip = 1 - 2 * b
    for s in range(lines - 1):
        lo = me - 2 * (s + 1)
        hi = me + 2 * (s + 1)

        @pl.when(lo >= 0)
        def _():
            arrived(1, lo + flip)

        @pl.when(hi < n)
        def _():
            arrived(1, hi + flip)

    base = pl.multiple_of(r * part, part)
    columns = p_ref.shape[0]
    for blk in range(n):
        total = lpart[blk, pl.ds(base, part), :]
        for k in range(1, n_row):
            ship_copy(blk, lax.rem(r + k, n_row), k).wait_recv()
            total = total + lrecv[k - 1, blk]
        lsum[:, blk * columns:(blk + 1) * columns] = total

    own_p.wait()
    own_q.wait()
    for blk in range(n):
        for k in range(1, n_row):
            ship_copy(blk, lax.rem(r + k, n_row), k).wait_send()
    for t in range(2):
        copy(t, 0, me, True).wait_send()

        @pl.when(a < lines - 1)
        def _():
            copy(t, 1, me, True).wait_send()

        @pl.when(a > 0)
        def _():
            copy(t, 2, me, True).wait_send()

        for s in range(lines - 1):
            lo = me - 2 * (s + 1)
            hi = me + 2 * (s + 1)

            @pl.when(lo >= 0)
            def _():
                copy(t, 0, lo).wait_send()

                @pl.when(a < lines - 1)
                def _():
                    copy(t, 1, lo).wait_send()

            @pl.when(hi < n)
            def _():
                copy(t, 0, hi).wait_send()

                @pl.when(a > 0)
                def _():
                    copy(t, 2, hi).wait_send()


def gather_and_logits(queries, passages, n, n_row):
    rows, width = queries.shape
    prows = passages.shape[0]
    part = rows // n_row
    vmem = pl.BlockSpec(memory_space=pltpu.VMEM)
    return pl.pallas_call(
        functools.partial(gather_kernel, n, n_row),
        name="gather_logits",
        out_shape=(
            jax.ShapeDtypeStruct((n, prows, width), passages.dtype),
            jax.ShapeDtypeStruct((n, rows, width), queries.dtype),
            jax.ShapeDtypeStruct((part, n * prows), jnp.float32),
        ),
        in_specs=[vmem, vmem],
        out_specs=(vmem, vmem, vmem),
        scratch_shapes=[
            pltpu.VMEM((n, rows, prows), jnp.float32),
            pltpu.VMEM((n_row - 1, n, part, prows), jnp.float32),
            pltpu.SemaphoreType.DMA((2, 3, n)),
            pltpu.SemaphoreType.DMA((2, n)),
            pltpu.SemaphoreType.DMA((n_row - 1, n)),
            pltpu.SemaphoreType.DMA((n_row - 1, n)),
            pltpu.SemaphoreType.DMA((2,)),
        ],
        compiler_params=pltpu.CompilerParams(
            collective_id=0, has_side_effects=True, vmem_limit_bytes=56 * 2**20
        ),
    )(queries, passages)


def weights_kernel(n, n_row, columns, w_ref, loss_ref, wrow, wcol, table, dsend, drecv, tsend,
                   trecv, rsend, rrecv, own_sem):
    me = lax.axis_index("dp")
    r = lax.axis_index("row")
    n_line = n_row // 2
    y = r // 2
    core = r % 2
    partner = y * 2 + 1 - core
    barrier = pltpu.get_barrier_semaphore()
    for j in range(1, n):
        pl.semaphore_signal(
            barrier, inc=1, device_id=(lax.rem(me + j, n), r), device_id_type=MESH
        )
    for k in range(1, n_line):
        pl.semaphore_signal(
            barrier, inc=1, device_id=(me, lax.rem(r + 2 * k, n_row)), device_id_type=MESH
        )
    pl.semaphore_signal(barrier, inc=1, device_id=(me, partner), device_id_type=MESH)
    pl.semaphore_wait(barrier, n + n_line - 1)

    def across(j):
        to = lax.rem(me + j, n)
        return pltpu.make_async_remote_copy(
            src_ref=w_ref.at[:, pl.ds(pl.multiple_of(to * columns, columns), columns)],
            dst_ref=wcol.at[y, core, me],
            send_sem=dsend.at[j - 1],
            recv_sem=drecv.at[j - 1],
            device_id=(to, r),
            device_id_type=MESH,
        )

    def tell(j):
        return pltpu.make_async_remote_copy(
            src_ref=loss_ref,
            dst_ref=table.at[y, core, me],
            send_sem=tsend.at[j - 1],
            recv_sem=trecv.at[j - 1],
            device_id=(lax.rem(me + j, n), r),
            device_id_type=MESH,
        )

    def along(which, k):
        out = (wrow, wcol, table)[which]
        return pltpu.make_async_remote_copy(
            src_ref=w_ref if which == 0 else out.at[y, core],
            dst_ref=out.at[y, core],
            send_sem=rsend.at[which, k - 1],
            recv_sem=rrecv.at[which, k - 1],
            device_id=(me, lax.rem(r + 2 * k, n_row)),
            device_id_type=MESH,
        )

    def beside(which):
        out = (wrow, wcol, table)[which]
        return pltpu.make_async_remote_copy(
            src_ref=out.at[:, core],
            dst_ref=out.at[:, core],
            send_sem=rsend.at[which, n_line - 1],
            recv_sem=rrecv.at[which, n_line - 1],
            device_id=(me, partner),
            device_id_type=MESH,
        )

    for j in range(1, n):
        across(j).start()
        tell(j).start()
    for k in range(1, n_line):
        along(0, k).start()
    owns = (
        pltpu.make_async_copy(w_ref, wrow.at[y, core], own_sem.at[0]),
        pltpu.make_async_copy(
            w_ref.at[:, pl.ds(pl.multiple_of(me * columns, columns), columns)],
            wcol.at[y, core, me],
            own_sem.at[1],
        ),
        pltpu.make_async_copy(loss_ref, table.at[y, core, me], own_sem.at[2]),
    )
    for own in owns:
        own.start()
    for own in owns:
        own.wait()
    for j in range(1, n):
        across(j).wait_recv()
        tell(j).wait_recv()
    for k in range(1, n_line):
        along(1, k).start()
        along(2, k).start()
    for which in range(3):
        for k in range(1, n_line):
            along(which, k).wait_recv()
        beside(which).start()
    for which in range(3):
        beside(which).wait_recv()
    for j in range(1, n):
        across(j).wait_send()
        tell(j).wait_send()
    for which in range(3):
        for k in range(1, n_line):
            along(which, k).wait_send()
        beside(which).wait_send()


def exchange_weights(weights_ext, loss_tile, n, n_row, columns):
    part, wide = weights_ext.shape
    vmem = pl.BlockSpec(memory_space=pltpu.VMEM)
    dma = pltpu.SemaphoreType.DMA
    n_line = n_row // 2
    return pl.pallas_call(
        functools.partial(weights_kernel, n, n_row, columns),
        name="exchange_weights",
        out_shape=(
            jax.ShapeDtypeStruct((n_line, 2, part, wide), weights_ext.dtype),
            jax.ShapeDtypeStruct((n_line, 2, n, part, columns), weights_ext.dtype),
            jax.ShapeDtypeStruct((n_line, 2, n) + loss_tile.shape, loss_tile.dtype),
        ),
        in_specs=[vmem, vmem],
        out_specs=(vmem, vmem, vmem),
        scratch_shapes=[
            dma((n - 1,)), dma((n - 1,)), dma((n - 1,)), dma((n - 1,)),
            dma((3, n_line)), dma((3, n_line)), dma((3,)),
        ],
        compiler_params=pltpu.CompilerParams(collective_id=1, has_side_effects=True),
    )(weights_ext, loss_tile)


def hard_kernel(n_row, x_ref, out, send, recv, own_sem):
    me = lax.axis_index("dp")
    r = lax.axis_index("row")
    barrier = pltpu.get_barrier_semaphore()
    for k in range(1, n_row):
        pl.semaphore_signal(
            barrier, inc=1, device_id=(me, lax.rem(r + k, n_row)), device_id_type=MESH
        )
    pl.semaphore_wait(barrier, n_row - 1)

    def along(k):
        return pltpu.make_async_remote_copy(
            src_ref=x_ref,
            dst_ref=out.at[r],
            send_sem=send.at[k - 1],
            recv_sem=recv.at[k - 1],
            device_id=(me, lax.rem(r + k, n_row)),
            device_id_type=MESH,
        )

    for k in range(1, n_row):
        along(k).start()
    own = pltpu.make_async_copy(x_ref, out.at[r], own_sem)
    own.start()
    own.wait()
    for k in range(1, n_row):
        along(k).wait()


def gather_hard(partial_hard, n_row):
    vmem = pl.BlockSpec(memory_space=pltpu.VMEM)
    dma = pltpu.SemaphoreType.DMA
    return pl.pallas_call(
        functools.partial(hard_kernel, n_row),
        name="gather_hard",
        out_shape=jax.ShapeDtypeStruct((n_row,) + partial_hard.shape, partial_hard.dtype),
        in_specs=[vmem],
        out_specs=vmem,
        scratch_shapes=[dma((n_row - 1,)), dma((n_row - 1,)), dma(())],
        compiler_params=pltpu.CompilerParams(collective_id=2, has_side_effects=True),
    )(partial_hard)


def softmax_rows(summed, summed_hard, sources, block_source, first_row, logit_scale):
    logits = logit_scale * summed
    hard_logits = logit_scale * summed_hard
    columns = jnp.arange(logits.shape[1], dtype=jnp.int32)
    targets = first_row + jnp.arange(logits.shape[0], dtype=jnp.int32)
    column_source = jnp.repeat(block_source, BLOCK)
    positive = columns[None, :] == targets[:, None]
    allowed = (sources[:, None] != column_source[None, :]) | positive
    masked = jnp.where(allowed, logits, NEG_FILL)
    maximum = jnp.maximum(jnp.max(masked, axis=1), jnp.max(hard_logits, axis=1))
    exponent = jnp.exp(masked - maximum[:, None])
    hard_expo = jnp.exp(hard_logits - maximum[:, None])
    totals = jnp.sum(exponent, axis=1) + jnp.sum(hard_expo, axis=1)
    pos_logit = jnp.sum(jnp.where(positive, logits, 0.0), axis=1)
    per_query = maximum + jnp.log(totals) - pos_logit
    weights = (exponent / totals[:, None] - positive.astype(jnp.float32)).astype(jnp.bfloat16)
    hard_weights = (hard_expo / totals[:, None]).astype(jnp.bfloat16)
    return (weights, hard_weights, jnp.sum(per_query))


def on_device(queries, passages, cached, hard_shard, hard_row, query_source, block_source):
    row_count, width = queries.shape
    columns = passages.shape[0]
    n_data = lax.axis_size("dp")
    n_row = lax.axis_size("row")
    part = row_count // n_row
    logit_scale = 1.0 / math.sqrt(D)
    hard_rows = fetch_hard(cached, hard_shard, hard_row, n_data)
    hard_count = hard_rows.shape[0]
    pall, qall, summed = gather_and_logits(queries, passages, n_data, n_row)
    partial_hard = jnp.sum(
        queries.astype(jnp.float32)[None] * hard_rows.astype(jnp.float32), axis=2
    )
    partial_hard = jnp.pad(partial_hard, ((0, -hard_count % 8), (0, 0)))
    summed_hard = jnp.sum(gather_hard(partial_hard, n_row), axis=0)[:hard_count]
    row_at = lax.axis_index("row") * part
    first_row = lax.axis_index("dp") * row_count + row_at
    my_hard = lax.dynamic_slice_in_dim(summed_hard, row_at, part, 1).T
    my_source = lax.dynamic_slice_in_dim(query_source, row_at, part, 0)
    weights, hard_weights, local_loss = softmax_rows(
        summed, my_hard, my_source, block_source, first_row, logit_scale
    )
    n_all = weights.shape[1]
    ext = jnp.concatenate(
        [weights, jnp.pad(hard_weights, ((0, 0), (0, LANES - hard_count)))], axis=1
    )
    loss_tile = jnp.full((8, LANES), local_loss, jnp.float32)
    wrow, wcol, losses = exchange_weights(ext, loss_tile, n_data, n_row, columns)
    loss_sum = jnp.sum(losses[:, :, :, 0, 0])
    mean_loss = loss_sum / (row_count * n_data)
    wrow = wrow.reshape(row_count, n_all + LANES)
    query_grad = jnp.dot(
        wrow[:, :n_all], pall.reshape(n_data * columns, width), preferred_element_type=jnp.float32
    )
    for h in range(hard_count):
        query_grad = query_grad + wrow[:, n_all + h:n_all + h + 1].astype(
            jnp.float32
        ) * hard_rows[h].astype(jnp.float32)
    passage_grad = lax.dot_general(
        wcol.reshape(n_row, n_data, part, columns),
        qall.reshape(n_data, n_row, part, width).transpose(1, 0, 2, 3),
        (((0, 1, 2), (0, 1, 2)), ((), ())),
        preferred_element_type=jnp.float32,
    )
    return (mean_loss, query_grad.astype(jnp.bfloat16), passage_grad.astype(jnp.bfloat16))


def fused_kernel(n, n_row, scale, sources_ref, note_ref, q_ref, p_ref, cache_ref,
                 qgrad, pgrad, loss_out,
                 qall, cache, picked, chosen, notes, lpart, cpart, ypart, peak, mass,
                 stat_own, stat_all, wts, acc, pacc, xsend, xrecv, zsend, zrecv,
                 loss_own, loss_all, loss_mine, loss_beside,
                 gsend, grecv, nsend, nrecv, csend, crecv, ysend, yrecv, ssend, srecv,
                 wsend, wrecv, xs, xr, zs, zr, lsend, lrecv, own_sem):
    me = lax.axis_index("dp")
    r = lax.axis_index("row")
    lines = n // 2
    a = me // 2
    b = me % 2
    n_line = n_row // 2
    y = r // 2
    core = r % 2
    across = a * 2 + 1 - b
    partner = y * 2 + 1 - core
    rows, width = q_ref.shape
    columns = p_ref.shape[0]
    half = rows // 2
    slots = cache.shape[0]
    tile = min(width, 256)
    f32 = jnp.float32
    bf16 = jnp.bfloat16

    load_cache = pltpu.make_async_copy(cache_ref, cache, own_sem.at[0])
    load_cache.start()
    own_q = pltpu.make_async_copy(q_ref, qall.at[me], own_sem.at[1])
    own_q.start()

    barrier = pltpu.get_barrier_semaphore()
    for j in range(1, n):
        pl.semaphore_signal(
            barrier, inc=1, device_id=(lax.rem(me + j, n), r), device_id_type=MESH
        )
    for k in range(1, n_line):
        pl.semaphore_signal(
            barrier, inc=1, device_id=(me, lax.rem(r + 2 * k, n_row)), device_id_type=MESH
        )
    pl.semaphore_signal(barrier, inc=1, device_id=(me, partner), device_id_type=MESH)
    pl.semaphore_wait(barrier, n + n_line - 1)

    def remote(src, dst, send, recv, to):
        return pltpu.make_async_remote_copy(
            src_ref=src, dst_ref=dst, send_sem=send, recv_sem=recv,
            device_id=to, device_id_type=MESH,
        )

    def query_copy(kind, blk, first=False):
        to = (across, me + 2, me - 2)[kind]
        return remote(
            q_ref if first else qall.at[blk], qall.at[blk],
            gsend.at[kind, blk], grecv.at[blk], (to, r),
        )

    def note_copy(j):
        to = lax.rem(me + j, n)
        return remote(
            note_ref.at[to], notes.at[me], nsend.at[j - 1], nrecv.at[j - 1], (to, r)
        )

    def core_copy(blk):
        return remote(
            lpart.at[blk, 1 - core], cpart.at[blk], csend.at[blk], crecv.at[blk], (me, partner)
        )

    def line_copy(blk, k):
        return remote(
            ypart.at[blk, y], ypart.at[blk, y], ysend.at[blk, k - 1], yrecv.at[blk, k - 1],
            (me, lax.rem(r + 2 * k, n_row)),
        )

    def stat_copy(j):
        to = lax.rem(me + j, n)
        return remote(stat_own, stat_all.at[me], ssend.at[j - 1], srecv.at[j - 1], (to, r))

    def weight_copy(blk):
        return remote(
            wts.at[blk, core], wts.at[blk, core], wsend.at[blk], wrecv.at[blk], (me, partner)
        )

    def cross_copy(zi):
        return remote(xsend.at[zi], xrecv.at[zi], xs.at[zi], xr.at[zi], (across, r))

    def up_copy(zi):
        return remote(zsend.at[zi], zrecv.at[zi], zs.at[zi], zr.at[zi], (me + 2, r))

    def down_copy(zi, last):
        slot = zi + last * (lines - zi)
        return remote(zsend.at[zi], zrecv.at[slot], zs.at[zi], zr.at[slot], (me - 2, r))

    def loss_copy(j):
        to = lax.rem(me + j, n)
        return remote(loss_own, loss_all.at[me], lsend.at[j - 1], lrecv.at[j - 1], (to, r))

    loss_core = remote(loss_mine, loss_beside, lsend.at[n - 1], lrecv.at[n - 1], (me, partner))

    def group(s, body):
        @pl.loop(0, 2)
        def _(k):
            zi = a + (2 * k - 1) * s

            @pl.when((zi >= 0) & (zi < lines) & (k + s > 0))
            def _():
                body(zi)

    lane = lax.broadcasted_iota(jnp.int32, (1, half), 1)
    sub = lax.broadcasted_iota(jnp.int32, (BLOCK, half), 0)
    at_lanes = pl.ds(pl.multiple_of(core * half, half), half)

    def pick(blk):
        wide = lax.broadcasted_iota(jnp.int32, (rows, rows), 0)
        high = lax.broadcasted_iota(jnp.int32, (rows, rows), 1)
        named = jnp.sum(
            jnp.where(wide == high, notes[blk, 0:1, :], 0.0), axis=1, keepdims=True
        )
        number = lax.broadcasted_iota(jnp.int32, (rows, slots), 1).astype(f32)
        chosen[...] = jnp.where(number == named, 1.0, 0.0).astype(bf16)
        for t in range(0, width, tile):
            picked[blk, :, t:t + tile] = jnp.dot(
                chosen[...], cache[:, t:t + tile], preferred_element_type=f32
            ).astype(bf16)

    over_width = (((1,), (1,)), ((), ()))
    over_rows = (((0,), (0,)), ((), ()))

    def multiply(blk):
        q = qall[blk]
        logits = lax.dot_general(p_ref[...], q, over_width, preferred_element_type=f32)
        for h in range(2):
            cut = slice(h * half, (h + 1) * half)
            mixed = lax.dot_general(
                picked[blk, cut, :], q[cut, :], over_width, preferred_element_type=f32
            )
            down = lax.broadcasted_iota(jnp.int32, (half, half), 0)
            right = lax.broadcasted_iota(jnp.int32, (half, half), 1)
            hard = jnp.sum(jnp.where(down == right, mixed, 0.0), axis=0, keepdims=True)
            lpart[blk, h, 0:columns, :] = logits[:, cut]
            lpart[blk, h, columns:columns + 8, :] = jnp.broadcast_to(hard, (8, half))
        core_copy(blk).start()

    def add_core(blk):
        core_copy(blk).wait_recv()
        ypart[blk, y] = lpart[blk, core] + cpart[blk]
        for k in range(1, n_line):
            line_copy(blk, k).start()

    def scored(blk, t):
        cut = slice(t * BLOCK, (t + 1) * BLOCK)
        values = scale * lpart[blk, core, cut, :]
        source = sources_ref[me * (columns // BLOCK) + t].astype(f32)
        positive = (sub + (me * columns + t * BLOCK)) == (lane + (blk * rows + core * half))
        allowed = (notes[blk, 1:2, at_lanes] != source) | positive
        return jnp.where(allowed, values, NEG_FILL), positive

    def scored_hard(blk):
        values = scale * lpart[blk, core, columns:columns + 1, :]
        return jnp.where(notes[blk, 0:1, at_lanes] >= 0.0, values, NEG_FILL)

    parts = columns // BLOCK

    def local_stats(blk):
        for k in range(1, n_line):
            line_copy(blk, k).wait_recv()
        total = ypart[blk, 0]
        for k in range(1, n_line):
            total = total + ypart[blk, k]
        lpart[blk, core] = total
        hard = scored_hard(blk)
        blocks = [scored(blk, t)[0] for t in range(parts)]
        top = hard
        for block in blocks:
            top = jnp.maximum(top, jnp.max(block, axis=0, keepdims=True))
        added = jnp.exp(hard - top)
        for block in blocks:
            added = added + jnp.sum(jnp.exp(block - top), axis=0, keepdims=True)
        stat_own[0, pl.ds(blk, 1), :] = top
        stat_own[1, pl.ds(blk, 1), :] = added

    @pl.when(a < lines - 1)
    def _():
        query_copy(1, me, True).start()

    @pl.when(a > 0)
    def _():
        query_copy(2, me, True).start()

    query_copy(0, me, True).start()
    for j in range(1, n):
        note_copy(j).start()
    notes[me] = note_ref[me]
    load_cache.wait()
    own_q.wait()
    for j in range(1, n):
        note_copy(j).wait_recv()

    def mine(f):
        return lambda zi: f(zi * 2 + b)

    def theirs(f):
        return lambda zi: f(zi * 2 + 1 - b)

    def relay(zi):
        blk = zi * 2 + b
        query_copy(0, blk).wait_recv()

        @pl.when((zi < a) & (a < lines - 1))
        def _():
            query_copy(1, blk).start()

        @pl.when((zi > a) & (a > 0))
        def _():
            query_copy(2, blk).start()

        query_copy(0, blk).start()

    def from_across(blk):
        query_copy(0, blk).wait_recv()
        multiply(blk)

    pick(me)
    multiply(me)
    group(1, mine(pick))
    pick(across)

    @pl.loop(1, lines)
    def _(s):
        group(s, relay)
        group(s, mine(multiply))
        group(s - 1, theirs(from_across))
        group(s - 1, mine(add_core))
        group(s - 1, theirs(add_core))

        @pl.when(s < lines - 1)
        def _():
            group(s + 1, mine(pick))

        group(s, theirs(pick))

        @pl.when(s > 1)
        def _():
            group(s - 2, mine(local_stats))
            group(s - 2, theirs(local_stats))

    if lines > 1:
        group(lines - 2, mine(local_stats))
        group(lines - 2, theirs(local_stats))
    group(lines - 1, mine(add_core))
    group(lines - 1, theirs(from_across))
    group(lines - 1, theirs(add_core))
    group(lines - 1, mine(local_stats))
    group(lines - 1, theirs(local_stats))

    for j in range(1, n):
        stat_copy(j).start()
    stat_all[me] = stat_own[...]
    for j in range(1, n):
        stat_copy(j).wait_recv()
    top = stat_all[0, 0]
    for j in range(1, n):
        top = jnp.maximum(top, stat_all[j, 0])
    total = stat_all[0, 1] * jnp.exp(stat_all[0, 0] - top)
    for j in range(1, n):
        total = total + stat_all[j, 1] * jnp.exp(stat_all[j, 0] - top)
    peak[...] = top
    mass[...] = total

    def weigh(blk):
        high = peak[pl.ds(blk, 1), :]
        whole = mass[pl.ds(blk, 1), :]
        for t in range(parts):
            masked, positive = scored(blk, t)
            weight = jnp.exp(masked - high) / whole - positive.astype(f32)
            wts[blk, core, t * BLOCK:(t + 1) * BLOCK, :] = weight.astype(bf16)
        hard = jnp.exp(scored_hard(blk) - high) / whole
        wts[blk, core, columns:columns + 16, :] = jnp.broadcast_to(hard, (16, half)).astype(bf16)
        weight_copy(blk).start()

    @pl.loop(0, lines)
    def _(k):
        group(lines - 1 - k, theirs(weigh))
        group(lines - 1 - k, mine(weigh))

    def gradient(blk, store):
        down = lax.broadcasted_iota(jnp.int32, (half, half), 0)
        right = lax.broadcasted_iota(jnp.int32, (half, half), 1)
        for h in range(2):
            hard = wts[blk, h, columns:columns + 1, :].astype(f32)
            diagonal = jnp.where(down == right, hard, 0.0).astype(bf16)
            cut = slice(h * half, (h + 1) * half)
            out = lax.dot_general(
                wts[blk, h, 0:columns, :], p_ref[...], over_rows, preferred_element_type=f32
            )
            out = out + jnp.dot(diagonal, picked[blk, cut, :], preferred_element_type=f32)
            store(cut, out)

    def send_across(zi):
        blk = zi * 2 + 1 - b
        weight_copy(blk).wait_recv()

        def store(cut, out):
            xsend[zi, cut, :] = out.astype(bf16)

        gradient(blk, store)
        cross_copy(zi).start()

    @pl.loop(0, lines)
    def _(k):
        group(lines - 1 - k, send_across)

    positive_logit = jnp.zeros((1, half), f32)
    for t in range(parts):
        masked, positive = scored(me, t)
        positive_logit = positive_logit + jnp.sum(
            jnp.where(positive, masked, 0.0), axis=0, keepdims=True
        )
    losses = peak[pl.ds(me, 1), :] + jnp.log(mass[pl.ds(me, 1), :]) - positive_logit
    loss_own[...] = jnp.broadcast_to(losses, (8, half))
    for j in range(1, n):
        loss_copy(j).start()
    loss_all[me] = loss_own[...]

    pacc[...] = jnp.zeros_like(pacc)

    def passage_terms(blk):
        both = jnp.concatenate([wts[blk, 0, 0:columns, :], wts[blk, 1, 0:columns, :]], axis=1)
        for t in range(0, width, tile):
            pacc[:, t:t + tile] += jnp.dot(
                both, qall[blk, :, t:t + tile], preferred_element_type=f32
            )

    def store_acc(cut, out):
        acc[cut, :] = out

    def pass_on(s):
        def body(zi):
            blk = zi * 2 + b
            weight_copy(blk).wait_recv()
            gradient(blk, store_acc)
            passage_terms(blk)
            passage_terms(zi * 2 + 1 - b)
            cross_copy(zi).wait_recv()
            acc[...] += xrecv[zi].astype(f32)

            @pl.when((zi > a) & (a > 0))
            def _():
                up_copy(zi).wait_recv()
                acc[...] += zrecv[zi].astype(f32)

            @pl.when((zi < a) & (a < lines - 1))
            def _():
                down_copy(zi, 0).wait_recv()
                acc[...] += zrecv[zi].astype(f32)

            zsend[zi] = acc[...].astype(bf16)

            @pl.when(zi > a)
            def _():
                up_copy(zi).start()

            @pl.when((zi < a) & (s == 1))
            def _():
                down_copy(zi, 1).start()

            @pl.when((zi < a) & (s > 1))
            def _():
                down_copy(zi, 0).start()

        return body

    @pl.loop(0, lines - 1)
    def _(k):
        s = lines - 1 - k
        group(s, pass_on(s))

    weight_copy(me).wait_recv()
    gradient(me, store_acc)
    passage_terms(me)
    passage_terms(across)
    pgrad[...] = pacc[...].astype(bf16)

    for j in range(1, n):
        loss_copy(j).wait_recv()
    sums = loss_all[0]
    for j in range(1, n):
        sums = sums + loss_all[j]
    loss_mine[...] = sums
    loss_core.start()
    loss_core.wait_recv()
    loss_out[...] = jnp.broadcast_to(
        jnp.sum(loss_mine[...] + loss_beside[...], axis=1, keepdims=True), (8, half)
    )

    cross_copy(a).wait_recv()
    acc[...] += xrecv[a].astype(f32)

    @pl.when(a > 0)
    def _():
        up_copy(a).wait_recv()
        acc[...] += zrecv[a].astype(f32)

    @pl.when(a < lines - 1)
    def _():
        down_copy(a, 1).wait_recv()
        acc[...] += zrecv[lines].astype(f32)

    qgrad[...] = acc[...].astype(bf16)

    query_copy(0, me, True).wait_send()

    @pl.when(a < lines - 1)
    def _():
        query_copy(1, me, True).wait_send()

    @pl.when(a > 0)
    def _():
        query_copy(2, me, True).wait_send()

    def sent(zi):
        blk = zi * 2 + b

        @pl.when((zi < a) & (a < lines - 1))
        def _():
            query_copy(1, blk).wait_send()

        @pl.when((zi > a) & (a > 0))
        def _():
            query_copy(2, blk).wait_send()

        query_copy(0, blk).wait_send()

        @pl.when(zi > a)
        def _():
            up_copy(zi).wait_send()

        @pl.when(zi < a)
        def _():
            down_copy(zi, 0).wait_send()

    @pl.loop(1, lines)
    def _(s):
        group(s, sent)

    @pl.loop(0, lines)
    def _(zi):
        cross_copy(zi).wait_send()

    @pl.loop(0, n)
    def _(blk):
        core_copy(blk).wait_send()
        weight_copy(blk).wait_send()
        for k in range(1, n_line):
            line_copy(blk, k).wait_send()

    for j in range(1, n):
        note_copy(j).wait_send()
        stat_copy(j).wait_send()
        loss_copy(j).wait_send()
    loss_core.wait_send()


def fused(queries, passages, cached, notes, block_source, n, n_row, scale):
    rows, width = queries.shape
    columns = passages.shape[0]
    slots = cached.shape[0]
    lines = n // 2
    n_line = n_row // 2
    half = rows // 2
    f32 = jnp.float32
    bf16 = jnp.bfloat16
    vmem = pl.BlockSpec(memory_space=pltpu.VMEM)
    mem = pltpu.VMEM
    dma = pltpu.SemaphoreType.DMA
    return pl.pallas_call(
        functools.partial(fused_kernel, n, n_row, scale),
        name="fused_loss",
        out_shape=(
            jax.ShapeDtypeStruct((rows, width), bf16),
            jax.ShapeDtypeStruct((columns, width), bf16),
            jax.ShapeDtypeStruct((8, half), f32),
        ),
        in_specs=[
            pl.BlockSpec(memory_space=pltpu.SMEM), vmem, vmem, vmem,
            pl.BlockSpec(memory_space=pl.ANY),
        ],
        out_specs=(vmem, vmem, vmem),
        scratch_shapes=[
            mem((n, rows, width), bf16),
            mem((slots, width), bf16),
            mem((n, rows, width), bf16),
            mem((rows, slots), bf16),
            mem((n, 2, rows), f32),
            mem((n, 2, columns + 8, half), f32),
            mem((n, columns + 8, half), f32),
            mem((n, n_line, columns + 8, half), f32),
            mem((n, half), f32),
            mem((n, half), f32),
            mem((2, n, half), f32),
            mem((n, 2, n, half), f32),
            mem((n, 2, columns + 16, half), bf16),
            mem((rows, width), f32),
            mem((columns, width), f32),
            mem((lines, rows, width), bf16),
            mem((lines, rows, width), bf16),
            mem((lines, rows, width), bf16),
            mem((lines + 1, rows, width), bf16),
            mem((8, half), f32),
            mem((n, 8, half), f32),
            mem((8, half), f32),
            mem((8, half), f32),
            dma((3, n)), dma((n,)),
            dma((n - 1,)), dma((n - 1,)),
            dma((n,)), dma((n,)),
            dma((n, max(n_line - 1, 1))), dma((n, max(n_line - 1, 1))),
            dma((n - 1,)), dma((n - 1,)),
            dma((n,)), dma((n,)),
            dma((lines,)), dma((lines,)),
            dma((lines,)), dma((lines + 1,)),
            dma((n,)), dma((n,)),
            dma((2,)),
        ],
        compiler_params=pltpu.CompilerParams(
            collective_id=0, has_side_effects=True, vmem_limit_bytes=60 * 2**20
        ),
    )(block_source, notes, queries, passages, cached)


def on_device_fused(queries, passages, cached, hard_shard, hard_row, query_source, block_source):
    n = lax.axis_size("dp")
    n_row = lax.axis_size("row")
    rows = queries.shape[0]
    shard = hard_shard.T[None]
    named = jnp.where(
        shard == jnp.arange(n, dtype=jnp.int32)[:, None, None], hard_row.T[None] + 1, 0
    )
    named = jnp.sum(named, axis=1) - 1
    notes = jnp.stack(
        [named, jnp.broadcast_to(query_source[None], (n, rows))], axis=1
    ).astype(jnp.float32)
    query_grad, passage_grad, losses = fused(
        queries, passages, cached, notes, block_source, n, n_row, 1.0 / math.sqrt(D)
    )
    return (losses[0, 0] / (rows * n), query_grad, passage_grad)


def fits(n, n_row, rows, width, slots):
    blocks = 2 * (n * rows * width * 2 + (2 * n + 2) * rows * width + slots * width)
    half = rows // 2
    scores = n * (3 + n_row // 2) * (rows + 8) * half * 4
    return blocks + scores < 48 * 2**20


def solution(mesh):
    in_specs = (
        P("dp", "row"),
        P("dp", "row"),
        P("dp", "row"),
        P("dp", None),
        P("dp", None),
        P("dp"),
        P(),
    )
    out_specs = (P(), P("dp", "row"), P("dp", "row"))

    def body(queries, passages, cached, *rest):
        rows, width = queries.shape
        n, n_row = mesh.shape["dp"], mesh.shape["row"]
        if fits(n, n_row, rows, width, cached.shape[0]):
            return on_device_fused(queries, passages, cached, *rest)
        return on_device(queries, passages, cached, *rest)

    return jax.shard_map(
        body, mesh=mesh, in_specs=in_specs, out_specs=out_specs, check_vma=False
    )
```

```python
import functools
import math

import jax
import jax.numpy as jnp
from jax import lax
from jax.experimental import pallas as pl
from jax.experimental.pallas import tpu as pltpu
from jax.sharding import PartitionSpec as P

D = 4096
BLOCK = 128
LANES = 128
NEG_FILL = -1e30
MESH = pl.DeviceIdType.MESH


def spill_kernel(n, hot, rows_ref, out, send, recv, own_sem):
    me = lax.axis_index("dp")
    r = lax.axis_index("row")
    barrier = pltpu.get_barrier_semaphore()

    def copy(j):
        to = (hot + j) % n
        return pltpu.make_async_remote_copy(
            src_ref=rows_ref.at[to],
            dst_ref=out,
            send_sem=send.at[j - 1],
            recv_sem=recv,
            device_id=(to, r),
            device_id_type=MESH,
        )

    @pl.when(me == hot)
    def _():
        for j in range(1, n):
            pl.semaphore_signal(
                barrier, inc=1, device_id=((hot + j) % n, r), device_id_type=MESH
            )

    @pl.when(me != hot)
    def _():
        pl.semaphore_signal(barrier, inc=1, device_id=(hot, r), device_id_type=MESH)

    pl.semaphore_wait(barrier, 1 + (me == hot).astype(jnp.int32) * (n - 2))

    @pl.when(me == hot)
    def _():
        for j in range(1, n):
            copy(j).start()
        own = pltpu.make_async_copy(rows_ref.at[hot], out, own_sem)
        own.start()
        own.wait()
        for j in range(1, n):
            copy(j).wait_send()

    @pl.when(me != hot)
    def _():
        copy(1).wait_recv()


def spill(n, hot, rows):
    vmem = pl.BlockSpec(memory_space=pltpu.VMEM)
    dma = pltpu.SemaphoreType.DMA
    return pl.pallas_call(
        functools.partial(spill_kernel, n, hot),
        name=f"spill_{hot}",
        out_shape=jax.ShapeDtypeStruct(rows.shape[1:], rows.dtype),
        in_specs=[vmem],
        out_specs=vmem,
        scratch_shapes=[dma((n - 1,)), dma(()), dma(())],
        compiler_params=pltpu.CompilerParams(collective_id=3 + hot, has_side_effects=True),
    )(rows)


def fetch_hard(cached, hard_shard, hard_row, n_data):
    row_count, hard_count = hard_shard.shape
    width_dev = cached.shape[1]
    capacity = min(row_count, 3 * row_count * hard_count // n_data)
    others = -(-(row_count * hard_count - capacity) // (n_data - 1))
    common = min(capacity - 16, -(-others // 16) * 16)
    owners = hard_shard.reshape(-1)
    wanted = hard_row.reshape(-1)
    one_hot = (owners[:, None] == jnp.arange(n_data, dtype=jnp.int32)[None, :]).astype(jnp.int32)
    before = jnp.cumsum(one_hot, axis=0) - one_hot
    slot_index = jnp.sum(before * one_hot, axis=1)
    hot = jnp.argmax(jnp.sum(one_hot, axis=0)).astype(jnp.int32)
    target = owners * capacity + slot_index
    requests = (
        jnp.zeros((n_data * capacity,), jnp.int32).at[target].set(wanted).reshape(n_data, capacity)
    )
    asked_rows = lax.all_to_all(requests, "dp", split_axis=0, concat_axis=0, tiled=True)
    picked = jnp.take(cached, asked_rows[:, :common].reshape(-1), axis=0, mode="clip")
    picked = picked.reshape(n_data, common, width_dev)
    replies = lax.all_to_all(picked, "dp", split_axis=0, concat_axis=0, tiled=True)
    extra = jnp.take(cached, asked_rows[:, common:].reshape(-1), axis=0, mode="clip")
    extra = extra.reshape(n_data, capacity - common, width_dev)
    spilled = lax.switch(hot, [functools.partial(spill, n_data, k) for k in range(n_data)], extra)
    reply_rows = jnp.concatenate([replies.reshape(n_data * common, width_dev), spilled], axis=0)
    place = jnp.where(
        slot_index < common, owners * common + slot_index, n_data * common + slot_index - common
    )
    by_slot = place.reshape(row_count, hard_count).T.reshape(-1)
    hard_rows = jnp.take(reply_rows, by_slot, axis=0, mode="clip")
    return hard_rows.reshape(hard_count, row_count, width_dev)


def gather_kernel(n, n_row, q_ref, p_ref, pall, qall, lsum, lpart, lrecv,
                  gsend, grecv, lsend, lrecv_sem, own_sem):
    me = lax.axis_index("dp")
    r = lax.axis_index("row")
    lines = n // 2
    a = me // 2
    b = me % 2
    rows = q_ref.shape[0]
    part = rows // n_row
    across = a * 2 + 1 - b

    barrier = pltpu.get_barrier_semaphore()
    pl.semaphore_signal(barrier, inc=1, device_id=(across, r), device_id_type=MESH)
    for k in range(1, n_row):
        pl.semaphore_signal(
            barrier, inc=1, device_id=(me, lax.rem(r + k, n_row)), device_id_type=MESH
        )

    @pl.when(a < lines - 1)
    def _():
        pl.semaphore_signal(barrier, inc=1, device_id=(me + 2, r), device_id_type=MESH)

    @pl.when(a > 0)
    def _():
        pl.semaphore_signal(barrier, inc=1, device_id=(me - 2, r), device_id_type=MESH)

    neighbours = (a < lines - 1).astype(jnp.int32) + (a > 0).astype(jnp.int32)
    pl.semaphore_wait(barrier, n_row + neighbours)

    alls = (pall, qall)
    own = (p_ref, q_ref)

    def copy(t, kind, blk, first=False):
        to = (across, me + 2, me - 2)[kind]
        return pltpu.make_async_remote_copy(
            src_ref=own[t] if first else alls[t].at[blk],
            dst_ref=alls[t].at[blk],
            send_sem=gsend.at[t, kind, blk],
            recv_sem=grecv.at[t, blk],
            device_id=(to, r),
            device_id_type=MESH,
        )

    def arrived(t, blk):
        copy(t, 0, blk).wait_recv()

    def start_own(t):
        @pl.when(a < lines - 1)
        def _():
            copy(t, 1, me, True).start()

        @pl.when(a > 0)
        def _():
            copy(t, 2, me, True).start()

        copy(t, 0, me, True).start()

    def multiply(blk, block):
        lpart[blk] = lax.dot_general(
            q_ref[...], block, (((1,), (1,)), ((), ())), preferred_element_type=jnp.float32
        )

    def ship(blk):
        for k in range(1, n_row):
            to = lax.rem(r + k, n_row)
            ship_copy(blk, to, k).start()

    def ship_copy(blk, to, k):
        return pltpu.make_async_remote_copy(
            src_ref=lpart.at[blk, pl.ds(pl.multiple_of(to * part, part), part), :],
            dst_ref=lrecv.at[k - 1, blk],
            send_sem=lsend.at[k - 1, blk],
            recv_sem=lrecv_sem.at[k - 1, blk],
            device_id=(me, to),
            device_id_type=MESH,
        )

    def relay(t, s):
        lo = me - 2 * (s + 1)
        hi = me + 2 * (s + 1)

        @pl.when(lo >= 0)
        def _():
            arrived(t, lo)

            @pl.when(a < lines - 1)
            def _():
                copy(t, 1, lo).start()

            copy(t, 0, lo).start()

        @pl.when(hi < n)
        def _():
            arrived(t, hi)

            @pl.when(a > 0)
            def _():
                copy(t, 2, hi).start()

            copy(t, 0, hi).start()

    def logits_of(s):
        lo = me - 2 * (s + 1)
        hi = me + 2 * (s + 1)
        flip = 1 - 2 * b

        @pl.when(lo >= 0)
        def _():
            multiply(lo, pall[lo])

        @pl.when(hi < n)
        def _():
            multiply(hi, pall[hi])

        @pl.when(lo >= 0)
        def _():
            ship(lo)
            arrived(0, lo + flip)
            multiply(lo + flip, pall[lo + flip])

        @pl.when(hi < n)
        def _():
            ship(hi)
            arrived(0, hi + flip)
            multiply(hi + flip, pall[hi + flip])

        @pl.when(lo >= 0)
        def _():
            ship(lo + flip)

        @pl.when(hi < n)
        def _():
            ship(hi + flip)

    start_own(0)
    own_p = pltpu.make_async_copy(p_ref, pall.at[me], own_sem.at[0])
    own_q = pltpu.make_async_copy(q_ref, qall.at[me], own_sem.at[1])
    own_p.start()
    own_q.start()
    multiply(me, p_ref[...])
    for s in range(lines - 1):
        relay(0, s)
        if s == lines - 2:
            start_own(1)
        if s == 0:
            ship(me)
            arrived(0, across)
            multiply(across, pall[across])
            ship(across)
        else:
            logits_of(s - 1)
    for s in range(lines - 1):
        relay(1, s)
        if s == 0:
            logits_of(lines - 2)
    arrived(1, across)
    flip = 1 - 2 * b
    for s in range(lines - 1):
        lo = me - 2 * (s + 1)
        hi = me + 2 * (s + 1)

        @pl.when(lo >= 0)
        def _():
            arrived(1, lo + flip)

        @pl.when(hi < n)
        def _():
            arrived(1, hi + flip)

    base = pl.multiple_of(r * part, part)
    columns = p_ref.shape[0]
    for blk in range(n):
        total = lpart[blk, pl.ds(base, part), :]
        for k in range(1, n_row):
            ship_copy(blk, lax.rem(r + k, n_row), k).wait_recv()
            total = total + lrecv[k - 1, blk]
        lsum[:, blk * columns:(blk + 1) * columns] = total

    own_p.wait()
    own_q.wait()
    for blk in range(n):
        for k in range(1, n_row):
            ship_copy(blk, lax.rem(r + k, n_row), k).wait_send()
    for t in range(2):
        copy(t, 0, me, True).wait_send()

        @pl.when(a < lines - 1)
        def _():
            copy(t, 1, me, True).wait_send()

        @pl.when(a > 0)
        def _():
            copy(t, 2, me, True).wait_send()

        for s in range(lines - 1):
            lo = me - 2 * (s + 1)
            hi = me + 2 * (s + 1)

            @pl.when(lo >= 0)
            def _():
                copy(t, 0, lo).wait_send()

                @pl.when(a < lines - 1)
                def _():
                    copy(t, 1, lo).wait_send()

            @pl.when(hi < n)
            def _():
                copy(t, 0, hi).wait_send()

                @pl.when(a > 0)
                def _():
                    copy(t, 2, hi).wait_send()


def gather_and_logits(queries, passages, n, n_row):
    rows, width = queries.shape
    prows = passages.shape[0]
    part = rows // n_row
    vmem = pl.BlockSpec(memory_space=pltpu.VMEM)
    return pl.pallas_call(
        functools.partial(gather_kernel, n, n_row),
        name="gather_logits",
        out_shape=(
            jax.ShapeDtypeStruct((n, prows, width), passages.dtype),
            jax.ShapeDtypeStruct((n, rows, width), queries.dtype),
            jax.ShapeDtypeStruct((part, n * prows), jnp.float32),
        ),
        in_specs=[vmem, vmem],
        out_specs=(vmem, vmem, vmem),
        scratch_shapes=[
            pltpu.VMEM((n, rows, prows), jnp.float32),
            pltpu.VMEM((n_row - 1, n, part, prows), jnp.float32),
            pltpu.SemaphoreType.DMA((2, 3, n)),
            pltpu.SemaphoreType.DMA((2, n)),
            pltpu.SemaphoreType.DMA((n_row - 1, n)),
            pltpu.SemaphoreType.DMA((n_row - 1, n)),
            pltpu.SemaphoreType.DMA((2,)),
        ],
        compiler_params=pltpu.CompilerParams(
            collective_id=0, has_side_effects=True, vmem_limit_bytes=56 * 2**20
        ),
    )(queries, passages)


def weights_kernel(n, n_row, columns, w_ref, loss_ref, wrow, wcol, table, dsend, drecv, tsend,
                   trecv, rsend, rrecv, own_sem):
    me = lax.axis_index("dp")
    r = lax.axis_index("row")
    n_line = n_row // 2
    y = r // 2
    core = r % 2
    partner = y * 2 + 1 - core
    barrier = pltpu.get_barrier_semaphore()
    for j in range(1, n):
        pl.semaphore_signal(
            barrier, inc=1, device_id=(lax.rem(me + j, n), r), device_id_type=MESH
        )
    for k in range(1, n_line):
        pl.semaphore_signal(
            barrier, inc=1, device_id=(me, lax.rem(r + 2 * k, n_row)), device_id_type=MESH
        )
    pl.semaphore_signal(barrier, inc=1, device_id=(me, partner), device_id_type=MESH)
    pl.semaphore_wait(barrier, n + n_line - 1)

    def across(j):
        to = lax.rem(me + j, n)
        return pltpu.make_async_remote_copy(
            src_ref=w_ref.at[:, pl.ds(pl.multiple_of(to * columns, columns), columns)],
            dst_ref=wcol.at[y, core, me],
            send_sem=dsend.at[j - 1],
            recv_sem=drecv.at[j - 1],
            device_id=(to, r),
            device_id_type=MESH,
        )

    def tell(j):
        return pltpu.make_async_remote_copy(
            src_ref=loss_ref,
            dst_ref=table.at[y, core, me],
            send_sem=tsend.at[j - 1],
            recv_sem=trecv.at[j - 1],
            device_id=(lax.rem(me + j, n), r),
            device_id_type=MESH,
        )

    def along(which, k):
        out = (wrow, wcol, table)[which]
        return pltpu.make_async_remote_copy(
            src_ref=w_ref if which == 0 else out.at[y, core],
            dst_ref=out.at[y, core],
            send_sem=rsend.at[which, k - 1],
            recv_sem=rrecv.at[which, k - 1],
            device_id=(me, lax.rem(r + 2 * k, n_row)),
            device_id_type=MESH,
        )

    def beside(which):
        out = (wrow, wcol, table)[which]
        return pltpu.make_async_remote_copy(
            src_ref=out.at[:, core],
            dst_ref=out.at[:, core],
            send_sem=rsend.at[which, n_line - 1],
            recv_sem=rrecv.at[which, n_line - 1],
            device_id=(me, partner),
            device_id_type=MESH,
        )

    for j in range(1, n):
        across(j).start()
        tell(j).start()
    for k in range(1, n_line):
        along(0, k).start()
    owns = (
        pltpu.make_async_copy(w_ref, wrow.at[y, core], own_sem.at[0]),
        pltpu.make_async_copy(
            w_ref.at[:, pl.ds(pl.multiple_of(me * columns, columns), columns)],
            wcol.at[y, core, me],
            own_sem.at[1],
        ),
        pltpu.make_async_copy(loss_ref, table.at[y, core, me], own_sem.at[2]),
    )
    for own in owns:
        own.start()
    for own in owns:
        own.wait()
    for j in range(1, n):
        across(j).wait_recv()
        tell(j).wait_recv()
    for k in range(1, n_line):
        along(1, k).start()
        along(2, k).start()
    for which in range(3):
        for k in range(1, n_line):
            along(which, k).wait_recv()
        beside(which).start()
    for which in range(3):
        beside(which).wait_recv()
    for j in range(1, n):
        across(j).wait_send()
        tell(j).wait_send()
    for which in range(3):
        for k in range(1, n_line):
            along(which, k).wait_send()
        beside(which).wait_send()


def exchange_weights(weights_ext, loss_tile, n, n_row, columns):
    part, wide = weights_ext.shape
    vmem = pl.BlockSpec(memory_space=pltpu.VMEM)
    dma = pltpu.SemaphoreType.DMA
    n_line = n_row // 2
    return pl.pallas_call(
        functools.partial(weights_kernel, n, n_row, columns),
        name="exchange_weights",
        out_shape=(
            jax.ShapeDtypeStruct((n_line, 2, part, wide), weights_ext.dtype),
            jax.ShapeDtypeStruct((n_line, 2, n, part, columns), weights_ext.dtype),
            jax.ShapeDtypeStruct((n_line, 2, n) + loss_tile.shape, loss_tile.dtype),
        ),
        in_specs=[vmem, vmem],
        out_specs=(vmem, vmem, vmem),
        scratch_shapes=[
            dma((n - 1,)), dma((n - 1,)), dma((n - 1,)), dma((n - 1,)),
            dma((3, n_line)), dma((3, n_line)), dma((3,)),
        ],
        compiler_params=pltpu.CompilerParams(collective_id=1, has_side_effects=True),
    )(weights_ext, loss_tile)


def hard_kernel(n_row, x_ref, out, send, recv, own_sem):
    me = lax.axis_index("dp")
    r = lax.axis_index("row")
    barrier = pltpu.get_barrier_semaphore()
    for k in range(1, n_row):
        pl.semaphore_signal(
            barrier, inc=1, device_id=(me, lax.rem(r + k, n_row)), device_id_type=MESH
        )
    pl.semaphore_wait(barrier, n_row - 1)

    def along(k):
        return pltpu.make_async_remote_copy(
            src_ref=x_ref,
            dst_ref=out.at[r],
            send_sem=send.at[k - 1],
            recv_sem=recv.at[k - 1],
            device_id=(me, lax.rem(r + k, n_row)),
            device_id_type=MESH,
        )

    for k in range(1, n_row):
        along(k).start()
    own = pltpu.make_async_copy(x_ref, out.at[r], own_sem)
    own.start()
    own.wait()
    for k in range(1, n_row):
        along(k).wait()


def gather_hard(partial_hard, n_row):
    vmem = pl.BlockSpec(memory_space=pltpu.VMEM)
    dma = pltpu.SemaphoreType.DMA
    return pl.pallas_call(
        functools.partial(hard_kernel, n_row),
        name="gather_hard",
        out_shape=jax.ShapeDtypeStruct((n_row,) + partial_hard.shape, partial_hard.dtype),
        in_specs=[vmem],
        out_specs=vmem,
        scratch_shapes=[dma((n_row - 1,)), dma((n_row - 1,)), dma(())],
        compiler_params=pltpu.CompilerParams(collective_id=2, has_side_effects=True),
    )(partial_hard)


def softmax_rows(summed, summed_hard, sources, block_source, first_row, logit_scale):
    logits = logit_scale * summed
    hard_logits = logit_scale * summed_hard
    columns = jnp.arange(logits.shape[1], dtype=jnp.int32)
    targets = first_row + jnp.arange(logits.shape[0], dtype=jnp.int32)
    column_source = jnp.repeat(block_source, BLOCK)
    positive = columns[None, :] == targets[:, None]
    allowed = (sources[:, None] != column_source[None, :]) | positive
    masked = jnp.where(allowed, logits, NEG_FILL)
    maximum = jnp.maximum(jnp.max(masked, axis=1), jnp.max(hard_logits, axis=1))
    exponent = jnp.exp(masked - maximum[:, None])
    hard_expo = jnp.exp(hard_logits - maximum[:, None])
    totals = jnp.sum(exponent, axis=1) + jnp.sum(hard_expo, axis=1)
    pos_logit = jnp.sum(jnp.where(positive, logits, 0.0), axis=1)
    per_query = maximum + jnp.log(totals) - pos_logit
    weights = (exponent / totals[:, None] - positive.astype(jnp.float32)).astype(jnp.bfloat16)
    hard_weights = (hard_expo / totals[:, None]).astype(jnp.bfloat16)
    return (weights, hard_weights, jnp.sum(per_query))


def on_device(queries, passages, cached, hard_shard, hard_row, query_source, block_source):
    row_count, width = queries.shape
    columns = passages.shape[0]
    n_data = lax.axis_size("dp")
    n_row = lax.axis_size("row")
    part = row_count // n_row
    logit_scale = 1.0 / math.sqrt(D)
    hard_rows = fetch_hard(cached, hard_shard, hard_row, n_data)
    hard_count = hard_rows.shape[0]
    pall, qall, summed = gather_and_logits(queries, passages, n_data, n_row)
    partial_hard = jnp.sum(
        queries.astype(jnp.float32)[None] * hard_rows.astype(jnp.float32), axis=2
    )
    partial_hard = jnp.pad(partial_hard, ((0, -hard_count % 8), (0, 0)))
    summed_hard = jnp.sum(gather_hard(partial_hard, n_row), axis=0)[:hard_count]
    row_at = lax.axis_index("row") * part
    first_row = lax.axis_index("dp") * row_count + row_at
    my_hard = lax.dynamic_slice_in_dim(summed_hard, row_at, part, 1).T
    my_source = lax.dynamic_slice_in_dim(query_source, row_at, part, 0)
    weights, hard_weights, local_loss = softmax_rows(
        summed, my_hard, my_source, block_source, first_row, logit_scale
    )
    n_all = weights.shape[1]
    ext = jnp.concatenate(
        [weights, jnp.pad(hard_weights, ((0, 0), (0, LANES - hard_count)))], axis=1
    )
    loss_tile = jnp.full((8, LANES), local_loss, jnp.float32)
    wrow, wcol, losses = exchange_weights(ext, loss_tile, n_data, n_row, columns)
    loss_sum = jnp.sum(losses[:, :, :, 0, 0])
    mean_loss = loss_sum / (row_count * n_data)
    wrow = wrow.reshape(row_count, n_all + LANES)
    query_grad = jnp.dot(
        wrow[:, :n_all], pall.reshape(n_data * columns, width), preferred_element_type=jnp.float32
    )
    for h in range(hard_count):
        query_grad = query_grad + wrow[:, n_all + h:n_all + h + 1].astype(
            jnp.float32
        ) * hard_rows[h].astype(jnp.float32)
    passage_grad = lax.dot_general(
        wcol.reshape(n_row, n_data, part, columns),
        qall.reshape(n_data, n_row, part, width).transpose(1, 0, 2, 3),
        (((0, 1, 2), (0, 1, 2)), ((), ())),
        preferred_element_type=jnp.float32,
    )
    return (mean_loss, query_grad.astype(jnp.bfloat16), passage_grad.astype(jnp.bfloat16))


def fused_kernel(n, n_row, stages, direct, scale, sources_ref, shard_ref, row_ref, source_ref,
                 q_ref, p_ref, cache_ref, qgrad, pgrad, loss_out,
                 qall, cache, picked, chosen, note_own, notes, unit_notes, lpart, cpart, ypart,
                 peak, mass, stat_own, stat_all, wts, acc, pacc, xsend, xrecv, zsend, zrecv,
                 lsum, lrest, loss_own, loss_all, loss_mine, loss_beside,
                 gsend, grecv, nsend, nrecv, csend, crecv, ysend, yrecv, ssend, srecv,
                 wsend, wrecv, xs, xr, zs, zr, ms, mr, lsend, lrecv, own_sem):
    me = lax.axis_index("dp")
    r = lax.axis_index("row")
    lines = n // 2
    far = lines - 1
    period = max(far, 1)
    a = me // 2
    b = me % 2
    n_line = n_row // 2
    y = r // 2
    core = r % 2
    across = a * 2 + 1 - b
    partner = y * 2 + 1 - core
    rows, width = q_ref.shape
    columns = p_ref.shape[0]
    parts = columns // BLOCK
    part = rows // stages
    pair = 2 * part
    rest = part - direct
    slots = cache.shape[0]
    tile = min(width, 256)
    f32 = jnp.float32
    bf16 = jnp.bfloat16

    load_cache = pltpu.make_async_copy(cache_ref, cache, own_sem.at[0])
    load_cache.start()

    barrier = pltpu.get_barrier_semaphore()
    for j in range(1, n):
        pl.semaphore_signal(
            barrier, inc=1, device_id=(lax.rem(me + j, n), r), device_id_type=MESH
        )
    for k in range(1, n_line):
        pl.semaphore_signal(
            barrier, inc=1, device_id=(me, lax.rem(r + 2 * k, n_row)), device_id_type=MESH
        )
    pl.semaphore_signal(barrier, inc=1, device_id=(me, partner), device_id_type=MESH)

    own_q = [
        pltpu.make_async_copy(
            q_ref.at[pl.ds(q * part, part)], qall.at[a, q, b], own_sem.at[1 + q]
        )
        for q in range(stages)
    ]
    for copy in own_q:
        copy.start()
    source = source_ref[...].astype(f32)
    for s in range(n):
        named = jnp.where(shard_ref[...] == s, row_ref[...] + 1, 0)
        note_own[s, 0:1, :] = jnp.sum(named.astype(f32), axis=0, keepdims=True) - 1.0
        note_own[s, 1:2, :] = source
    pacc[...] = jnp.zeros_like(pacc)
    lsum[...] = jnp.zeros_like(lsum)
    stat_own[...] = jnp.zeros_like(stat_own)
    pl.semaphore_wait(barrier, n + n_line - 1)

    def remote(src, dst, send, recv, to):
        return pltpu.make_async_remote_copy(
            src_ref=src, dst_ref=dst, send_sem=send, recv_sem=recv,
            device_id=to, device_id_type=MESH,
        )

    head = pl.ds(0, direct)
    tail = pl.ds(direct, rest)

    def own_rows(q, start, size):
        return q_ref.at[pl.ds(pl.multiple_of(q * part + start, 16), size)]

    def column_copy(up, zi, q, first=False):
        at = qall.at[zi, q, b]
        return remote(
            own_rows(q, 0, part) if first else at, at, gsend.at[1 if up else 2, zi, q],
            grecv.at[0, zi, q], (me + 2 if up else me - 2, r),
        )

    def head_copy(zi, q, first=False):
        at = qall.at[zi, q, b, head]
        return remote(
            own_rows(q, 0, direct) if first else at, at, gsend.at[0, zi, q],
            grecv.at[1, zi, q], (across, r),
        )

    def tail_copy(q):
        return remote(
            own_rows(q, direct, rest), qall.at[a, q, b, tail], gsend.at[3, a, q],
            grecv.at[2, a, q], (across, r),
        )

    def tail_relay(up, zi, q):
        at = qall.at[zi, q, 1 - b, tail]
        return remote(
            at, at, gsend.at[4 if up else 5, zi, q], grecv.at[2, zi, q],
            (me + 2 if up else me - 2, r),
        )

    def note_copy(j):
        to = lax.rem(me + j, n)
        return remote(
            note_own.at[to], notes.at[me], nsend.at[j - 1], nrecv.at[j - 1], (to, r)
        )

    def core_copy(zi, q):
        return remote(
            lpart.at[q, zi], cpart.at[q, zi // 2], csend.at[q, zi], crecv.at[q, zi],
            (me, partner),
        )

    def line_copy(zi, q, k):
        at = ypart.at[q, zi // 2, y]
        return remote(
            at, at, ysend.at[q, zi, k - 1], yrecv.at[q, zi, k - 1],
            (me, lax.rem(r + 2 * k, n_row)),
        )

    def stat_copy(j, q):
        to = lax.rem(me + j, n)
        return remote(
            stat_own.at[q], stat_all.at[q, me], ssend.at[q, j - 1], srecv.at[q, j - 1], (to, r)
        )

    def weight_copy(zi, q):
        at = wts.at[q, zi]
        return remote(at, at, wsend.at[q, zi], wrecv.at[q, zi], (me, partner))

    def cross_copy(zi, q):
        return remote(xsend.at[q, zi], xrecv.at[q, zi], xs.at[q, zi], xr.at[q, zi], (across, r))

    def up_copy(zi, q):
        return remote(zsend.at[q, zi], zrecv.at[q, zi], zs.at[q, zi], zr.at[q, zi], (me + 2, r))

    def down_copy(zi, q, last):
        slot = zi + last * (lines - zi)
        return remote(
            zsend.at[q, zi], zrecv.at[q, slot], zs.at[q, zi], zr.at[q, slot], (me - 2, r)
        )

    def rest_copy(q):
        return remote(zsend.at[q, a, pl.ds(part, rest)], lrest.at[q], ms.at[q], mr.at[q], (across, r))

    def loss_copy(j):
        to = lax.rem(me + j, n)
        return remote(loss_own, loss_all.at[me], lsend.at[j - 1], lrecv.at[j - 1], (to, r))

    loss_core = remote(loss_mine, loss_beside, lsend.at[n - 1], lrecv.at[n - 1], (me, partner))

    def group(s, body):
        if s == 0:
            body(a)
            return

        @pl.loop(0, 2)
        def _(k):
            zi = a + (2 * k - 1) * s

            @pl.when((zi >= 0) & (zi < lines))
            def _():
                body(zi)

    def owned(body):
        def f(zi):
            @pl.when(zi % 2 == core)
            def _():
                body(zi)

        return f

    lane = lax.broadcasted_iota(jnp.int32, (1, pair), 1)
    right_half = (lane >= part).astype(jnp.int32)
    sub = lax.broadcasted_iota(jnp.int32, (BLOCK, pair), 0)
    over_width = (((1,), (1,)), ((), ()))
    over_rows = (((0,), (0,)), ((), ()))

    def diagonal():
        down = lax.broadcasted_iota(jnp.int32, (pair, pair), 0)
        right = lax.broadcasted_iota(jnp.int32, (pair, pair), 1)
        return down == right

    def start_own(q):
        @pl.when(a < far)
        def _():
            column_copy(True, a, q, True).start()

        @pl.when(a > 0)
        def _():
            column_copy(False, a, q, True).start()

        tail_copy(q).start()
        head_copy(a, q, True).start()

    def turn(q):
        tail_copy(q).wait_recv()

        @pl.when(a < far)
        def _():
            tail_relay(True, a, q).start()

        @pl.when(a > 0)
        def _():
            tail_relay(False, a, q).start()

    def relay(s):
        def column(q):
            def body(zi):
                column_copy(True, zi, q).wait_recv()

                @pl.when((zi < a) & (a < far))
                def _():
                    column_copy(True, zi, q).start()

                @pl.when((zi > a) & (a > 0))
                def _():
                    column_copy(False, zi, q).start()

                head_copy(zi, q).start()

            return body

        def tails(q):
            def body(zi):
                tail_relay(True, zi, q).wait_recv()

                @pl.when((zi < a) & (a < far))
                def _():
                    tail_relay(True, zi, q).start()

                @pl.when((zi > a) & (a > 0))
                def _():
                    tail_relay(False, zi, q).start()

            return body

        def run(q):
            group(s, column(q))
            group(s, tails(q))

        return run

    def pick(s):
        def run(q):
            @pl.when(q % 2 == 0)
            def _():
                def body(zi):
                    named = jnp.concatenate(
                        [unit_notes[zi, q, 0:1, :], unit_notes[zi, q + 1, 0:1, :]], axis=1
                    )
                    down = lax.broadcasted_iota(jnp.int32, (2 * pair, 2 * pair), 0)
                    right = lax.broadcasted_iota(jnp.int32, (2 * pair, 2 * pair), 1)
                    named = jnp.sum(
                        jnp.where(down == right, named, 0.0), axis=1, keepdims=True
                    )
                    number = lax.broadcasted_iota(jnp.int32, (2 * pair, slots), 1).astype(f32)
                    chosen[...] = jnp.where(number == named, 1.0, 0.0).astype(bf16)
                    for t in range(0, width, tile):
                        found = jnp.dot(
                            chosen[...], cache[:, t:t + tile], preferred_element_type=f32
                        ).astype(bf16)
                        picked[zi, q, :, t:t + tile] = found[:pair]
                        picked[zi, q + 1, :, t:t + tile] = found[pair:]

                group(s, body)

        return run

    def multiply(s):
        def run(q):
            def body(zi):
                head_copy(zi, q).wait_recv()
                queries = qall[zi, q].reshape(pair, width)
                lpart[q, zi, 0:columns, :] = lax.dot_general(
                    p_ref[...], queries, over_width, preferred_element_type=f32
                )
                mixed = lax.dot_general(
                    picked[zi, q], queries, over_width, preferred_element_type=f32
                )
                hard = jnp.sum(jnp.where(diagonal(), mixed, 0.0), axis=0, keepdims=True)
                lpart[q, zi, columns:columns + 8, :] = jnp.broadcast_to(hard, (8, pair))

                @pl.when(zi % 2 != core)
                def _():
                    core_copy(zi, q).start()

            group(s, body)

        return run

    def add_core(s):
        def run(q):
            def body(zi):
                core_copy(zi, q).wait_recv()
                ypart[q, zi // 2, y] = lpart[q, zi] + cpart[q, zi // 2]
                for k in range(1, n_line):
                    line_copy(zi, q, k).start()

            group(s, owned(body))

        return run

    def scored(zi, q, t):
        values = scale * lpart[q, zi, t * BLOCK:(t + 1) * BLOCK, :]
        block = sources_ref[me * parts + t].astype(f32)
        query = (zi * 2 + right_half) * rows + q * part + lane - right_half * part
        positive = (sub + (me * columns + t * BLOCK)) == query
        allowed = (unit_notes[zi, q, 1:2, :] != block) | positive
        return jnp.where(allowed, values, NEG_FILL), positive

    def scored_hard(zi, q):
        values = scale * lpart[q, zi, columns:columns + 1, :]
        return jnp.where(unit_notes[zi, q, 0:1, :] >= 0.0, values, NEG_FILL)

    def local_stats(s):
        def run(q):
            def body(zi):
                for k in range(1, n_line):
                    line_copy(zi, q, k).wait_recv()
                total = ypart[q, zi // 2, 0]
                for k in range(1, n_line):
                    total = total + ypart[q, zi // 2, k]
                lpart[q, zi] = total
                hard = scored_hard(zi, q)
                blocks = [scored(zi, q, t)[0] for t in range(parts)]
                top = hard
                for block in blocks:
                    top = jnp.maximum(top, jnp.max(block, axis=0, keepdims=True))
                added = jnp.exp(hard - top)
                for block in blocks:
                    added = added + jnp.sum(jnp.exp(block - top), axis=0, keepdims=True)
                stat_own[q, 0, pl.ds(zi // 2, 1), :] = top
                stat_own[q, 1, pl.ds(zi // 2, 1), :] = added

            group(s, owned(body))
            if s == far:
                for j in range(1, n):
                    stat_copy(j, q).start()
                stat_all[q, me] = stat_own[q]

        return run

    def weigh(q):
        for j in range(1, n):
            stat_copy(j, q).wait_recv()
        top = stat_all[q, 0, 0]
        for j in range(1, n):
            top = jnp.maximum(top, stat_all[q, j, 0])
        total = stat_all[q, 0, 1] * jnp.exp(stat_all[q, 0, 0] - top)
        for j in range(1, n):
            total = total + stat_all[q, j, 1] * jnp.exp(stat_all[q, j, 0] - top)
        peak[...] = top
        mass[...] = total

        def body(zi):
            high = peak[pl.ds(zi // 2, 1), :]
            whole = mass[pl.ds(zi // 2, 1), :]
            own_logit = jnp.zeros((1, pair), f32)
            for t in range(parts):
                masked, positive = scored(zi, q, t)
                weight = jnp.exp(masked - high) / whole - positive.astype(f32)
                wts[q, zi, t * BLOCK:(t + 1) * BLOCK, :] = weight.astype(bf16)
                own_logit = own_logit + jnp.sum(
                    jnp.where(positive, masked, 0.0), axis=0, keepdims=True
                )
            hard = jnp.exp(scored_hard(zi, q) - high) / whole
            wts[q, zi, columns:columns + 16, :] = jnp.broadcast_to(hard, (16, pair)).astype(bf16)
            weight_copy(zi, q).start()
            counted = ((zi * 2 + right_half) == me).astype(jnp.int32) > 0
            lsum[...] += jnp.where(counted, high + jnp.log(whole) - own_logit, 0.0)

        @pl.loop(0, lines)
        def _(zi):
            owned(body)(zi)

    def send_across(q):
        def body(zi):
            @pl.when(zi % 2 != core)
            def _():
                weight_copy(zi, q).wait_recv()

            hard = wts[q, zi, columns:columns + 1, :].astype(f32)
            chooser = jnp.where(diagonal(), hard, 0.0).astype(bf16)
            for t in range(0, width, tile):
                out = lax.dot_general(
                    wts[q, zi, 0:columns, :], p_ref[:, t:t + tile], over_rows,
                    preferred_element_type=f32,
                )
                acc[q % 2, zi, :, t:t + tile] = out + jnp.dot(
                    chooser, picked[zi, q, :, t:t + tile], preferred_element_type=f32
                )
            other = pl.ds(pl.multiple_of((1 - b) * part, part), direct)
            xsend[q, zi] = acc[q % 2, zi, other, :].astype(bf16)
            cross_copy(zi, q).start()

        for s in range(far, -1, -1):
            group(s, body)

    mine = pl.ds(pl.multiple_of(b * part, part), part)
    mine_head = pl.ds(pl.multiple_of(b * part, part), direct)
    mine_tail = pl.ds(pl.multiple_of(b * part + direct, 16), rest)
    other_tail = pl.ds(pl.multiple_of((1 - b) * part + direct, 16), rest)

    def add_line(zi, q, slot):
        acc[q % 2, zi, mine, :] += zrecv[q, slot, 0:part, :].astype(f32)
        acc[q % 2, zi, other_tail, :] += zrecv[q, slot, part:part + rest, :].astype(f32)

    def pass_on(s):
        def run(q):
            def body(zi):
                cross_copy(zi, q).wait_recv()
                acc[q % 2, zi, mine_head, :] += xrecv[q, zi].astype(f32)

                @pl.when(((zi > a) & (a > 0)) | ((zi < a) & (a < far)))
                def _():
                    up_copy(zi, q).wait_recv()
                    add_line(zi, q, zi)

                zsend[q, zi, 0:part, :] = acc[q % 2, zi, mine, :].astype(bf16)
                zsend[q, zi, part:part + rest, :] = acc[q % 2, zi, other_tail, :].astype(bf16)

                @pl.when(zi > a)
                def _():
                    up_copy(zi, q).start()

                @pl.when(zi < a)
                def _():
                    down_copy(zi, q, int(s == 1)).start()

            group(s, body)

        return run

    def gather_own(q):
        cross_copy(a, q).wait_recv()
        acc[q % 2, a, mine_head, :] += xrecv[q, a].astype(f32)

        @pl.when(a > 0)
        def _():
            up_copy(a, q).wait_recv()
            add_line(a, q, a)

        @pl.when(a < far)
        def _():
            down_copy(a, q, 1).wait_recv()
            add_line(a, q, lines)

        zsend[q, a, part:part + rest, :] = acc[q % 2, a, other_tail, :].astype(bf16)
        rest_copy(q).start()

    def finish(q):
        rest_copy(q).wait_recv()
        acc[q % 2, a, mine_tail, :] += lrest[q].astype(f32)
        qgrad[pl.ds(pl.multiple_of(q * part, part), part), :] = acc[q % 2, a, mine, :].astype(bf16)

    def passage_terms(q):
        for t in range(0, width, tile):
            total = pacc[:, t:t + tile]
            for zi in range(lines):
                total = total + jnp.dot(
                    wts[q, zi, 0:columns, :],
                    qall[zi, q, :, :, t:t + tile].reshape(pair, tile),
                    preferred_element_type=f32,
                )
            pacc[:, t:t + tile] = total

    def tell_loss(q):
        @pl.when(q == stages - 1)
        def _():
            loss_own[...] = jnp.broadcast_to(lsum[...], (8, pair))
            for j in range(1, n):
                loss_copy(j).start()
            loss_all[me] = loss_own[...]

    start_own(0)
    for j in range(1, n):
        note_copy(j).start()
    notes[me] = note_own[me]
    for j in range(1, n):
        note_copy(j).wait_recv()

    @pl.loop(0, lines)
    def _(zi):
        for q in range(stages):
            cut = slice(q * part, (q + 1) * part)
            unit_notes[zi, q] = jnp.concatenate(
                [notes[zi * 2, :, cut], notes[zi * 2 + 1, :, cut]], axis=1
            )

    load_cache.wait()
    for copy in own_q:
        copy.wait()

    acts = [(1, turn)]
    acts += [(s, relay(s)) for s in range(1, lines)]
    acts += [(period, lambda q: pl.when(q < stages - 1)(lambda: start_own(q + 1)))]
    acts += [(2 * far + 5 - s, pass_on(s)) for s in range(1, lines)]
    acts += [(2 * far + 5, gather_own), (2 * far + 6, finish)]
    acts += [(far + 4, weigh)]
    acts += [(s + 3, local_stats(s)) for s in range(lines)]
    acts += [(s + 2, add_core(s)) for s in range(lines)]
    acts += [(max(s - 1, 0), pick(s)) for s in range(lines)]
    acts += [(s + 1, multiply(s)) for s in range(lines)]
    acts += [(far + 4, send_across), (far + 5, tell_loss), (far + 6, passage_terms)]
    depth = max(o for o, _ in acts) // period

    @pl.loop(0, stages + depth)
    def _(turn_at):
        for j in range(period):
            for o, act in acts:
                if o % period == j:
                    q = turn_at - o // period

                    @pl.when((q >= 0) & (q < stages))
                    def _():
                        act(q)

    pgrad[...] = pacc[...].astype(bf16)
    for j in range(1, n):
        loss_copy(j).wait_recv()
    sums = loss_all[0]
    for j in range(1, n):
        sums = sums + loss_all[j]
    loss_mine[...] = sums
    loss_core.start()
    loss_core.wait_recv()
    loss_out[...] = jnp.broadcast_to(
        jnp.sum(loss_mine[...] + loss_beside[...], axis=1, keepdims=True), (8, pair)
    )

    def sent(zi, q):
        @pl.when((zi <= a) & (a < far))
        def _():
            column_copy(True, zi, q).wait_send()
            tail_relay(True, zi, q).wait_send()

        @pl.when((zi >= a) & (a > 0))
        def _():
            column_copy(False, zi, q).wait_send()
            tail_relay(False, zi, q).wait_send()

        head_copy(zi, q).wait_send()
        cross_copy(zi, q).wait_send()

        @pl.when(zi != a)
        def _():
            up_copy(zi, q).wait_send()

        @pl.when(zi % 2 != core)
        def _():
            core_copy(zi, q).wait_send()

        @pl.when(zi % 2 == core)
        def _():
            weight_copy(zi, q).wait_send()
            for k in range(1, n_line):
                line_copy(zi, q, k).wait_send()

    @pl.loop(0, stages)
    def _(q):
        @pl.loop(0, lines)
        def _(zi):
            sent(zi, q)

        tail_copy(q).wait_send()
        rest_copy(q).wait_send()
        for j in range(1, n):
            stat_copy(j, q).wait_send()

    for j in range(1, n):
        note_copy(j).wait_send()
        loss_copy(j).wait_send()
    loss_core.wait_send()


def fused(queries, passages, cached, shard, row, source, block_source, n, n_row, scale):
    rows, width = queries.shape
    columns = passages.shape[0]
    slots = cached.shape[0]
    lines = n // 2
    n_line = n_row // 2
    pair = LANES
    part = pair // 2
    stages = rows // part
    direct = part * 3 // 4
    rest = part - direct
    held = (lines + 1) // 2
    f32 = jnp.float32
    bf16 = jnp.bfloat16
    vmem = pl.BlockSpec(memory_space=pltpu.VMEM)
    mem = pltpu.VMEM
    dma = pltpu.SemaphoreType.DMA
    wires = max(n_line - 1, 1)
    return pl.pallas_call(
        functools.partial(fused_kernel, n, n_row, stages, direct, scale),
        name="fused_loss",
        out_shape=(
            jax.ShapeDtypeStruct((rows, width), bf16),
            jax.ShapeDtypeStruct((columns, width), bf16),
            jax.ShapeDtypeStruct((8, pair), f32),
        ),
        in_specs=[
            pl.BlockSpec(memory_space=pltpu.SMEM), vmem, vmem, vmem, vmem, vmem,
            pl.BlockSpec(memory_space=pl.ANY),
        ],
        out_specs=(vmem, vmem, vmem),
        scratch_shapes=[
            mem((lines, stages, 2, part, width), bf16),
            mem((slots, width), bf16),
            mem((lines, stages, pair, width), bf16),
            mem((2 * pair, slots), bf16),
            mem((n, 2, rows), f32),
            mem((n, 2, rows), f32),
            mem((lines, stages, 2, pair), f32),
            mem((stages, lines, columns + 8, pair), f32),
            mem((stages, held, columns + 8, pair), f32),
            mem((stages, held, n_line, columns + 8, pair), f32),
            mem((held, pair), f32),
            mem((held, pair), f32),
            mem((stages, 2, held, pair), f32),
            mem((stages, n, 2, held, pair), f32),
            mem((stages, lines, columns + 16, pair), bf16),
            mem((2, lines, pair, width), f32),
            mem((columns, width), f32),
            mem((stages, lines, direct, width), bf16),
            mem((stages, lines, direct, width), bf16),
            mem((stages, lines, part + rest, width), bf16),
            mem((stages, lines + 1, part + rest, width), bf16),
            mem((1, pair), f32),
            mem((stages, rest, width), bf16),
            mem((8, pair), f32),
            mem((n, 8, pair), f32),
            mem((8, pair), f32),
            mem((8, pair), f32),
            dma((6, lines, stages)), dma((3, lines, stages)),
            dma((n - 1,)), dma((n - 1,)),
            dma((stages, lines)), dma((stages, lines)),
            dma((stages, lines, wires)), dma((stages, lines, wires)),
            dma((stages, n - 1)), dma((stages, n - 1)),
            dma((stages, lines)), dma((stages, lines)),
            dma((stages, lines)), dma((stages, lines)),
            dma((stages, lines)), dma((stages, lines + 1)),
            dma((stages,)), dma((stages,)),
            dma((n,)), dma((n,)),
            dma((1 + stages,)),
        ],
        compiler_params=pltpu.CompilerParams(
            collective_id=0, has_side_effects=True, vmem_limit_bytes=56 * 2**20
        ),
    )(block_source, shard, row, source, queries, passages, cached)


def hand_out_kernel(share, q_ref, p_ref, loss_ref, q_out, p_out, loss_out, held, in_sem, out_sem):
    chunks = in_sem.shape[1]
    size = q_ref.shape[0] // chunks
    pairs = ((q_ref, q_out), (p_ref, p_out))

    def take(t, k):
        at = pl.ds(k * size, size)
        return pltpu.make_async_copy(pairs[t][0].at[at], held.at[t, at], in_sem.at[t, k])

    def give(t, k):
        at = pl.ds(k * size, size)
        return pltpu.make_async_copy(held.at[t, at], pairs[t][1].at[at], out_sem.at[t, k])

    for k in range(chunks):
        for t in range(2):
            take(t, k).start()
    loss_out[0, 0] = share * jnp.sum(loss_ref[0:1, 0:1])
    for k in range(chunks):
        for t in range(2):
            take(t, k).wait()
            give(t, k).start()
    for k in range(chunks):
        for t in range(2):
            give(t, k).wait()


def hand_out(query_grad, passage_grad, losses, share):
    rows, width = query_grad.shape
    vmem = pl.BlockSpec(memory_space=pltpu.VMEM)
    any_space = pl.BlockSpec(memory_space=pl.ANY)
    dma = pltpu.SemaphoreType.DMA
    chunks = 4
    return pl.pallas_call(
        functools.partial(hand_out_kernel, share),
        name="hand_out",
        out_shape=(
            jax.ShapeDtypeStruct(query_grad.shape, query_grad.dtype),
            jax.ShapeDtypeStruct(passage_grad.shape, passage_grad.dtype),
            jax.ShapeDtypeStruct((1, 1), jnp.float32),
        ),
        in_specs=[any_space, any_space, vmem],
        out_specs=(any_space, any_space, pl.BlockSpec(memory_space=pltpu.SMEM)),
        scratch_shapes=[
            pltpu.VMEM((2, rows, width), query_grad.dtype),
            dma((2, chunks)), dma((2, chunks)),
        ],
    )(query_grad, passage_grad, losses)


def on_device_fused(queries, passages, cached, hard_shard, hard_row, query_source, block_source):
    n = lax.axis_size("dp")
    n_row = lax.axis_size("row")
    rows = queries.shape[0]
    query_grad, passage_grad, losses = fused(
        queries, passages, cached, hard_shard.T, hard_row.T, query_source.reshape(1, rows),
        block_source, n, n_row, 1.0 / math.sqrt(D)
    )
    query_grad, passage_grad, loss = hand_out(
        query_grad, passage_grad, losses, 1.0 / (rows * n)
    )
    return (loss.reshape(()), query_grad, passage_grad)


def fits(n, n_row, rows, width, slots):
    blocks = 2 * (n * rows * width * 2 + (2 * n + 2) * rows * width + slots * width)
    half = rows // 2
    scores = n * (3 + n_row // 2) * (rows + 8) * half * 4
    return blocks + scores < 48 * 2**20


def solution(mesh):
    in_specs = (
        P("dp", "row"),
        P("dp", "row"),
        P("dp", "row"),
        P("dp", None),
        P("dp", None),
        P("dp"),
        P(),
    )
    out_specs = (P(), P("dp", "row"), P("dp", "row"))

    def body(queries, passages, cached, *rest):
        rows, width = queries.shape
        n, n_row = mesh.shape["dp"], mesh.shape["row"]
        if fits(n, n_row, rows, width, cached.shape[0]):
            return on_device_fused(queries, passages, cached, *rest)
        return on_device(queries, passages, cached, *rest)

    return jax.shard_map(
        body, mesh=mesh, in_specs=in_specs, out_specs=out_specs, check_vma=False
    )
```

```python
import functools
import math

import jax
import jax.numpy as jnp
from jax import lax
from jax.experimental import pallas as pl
from jax.experimental.pallas import tpu as pltpu
from jax.sharding import PartitionSpec as P

D = 4096
BLOCK = 128
LANES = 128
NEG_FILL = -1e30
MESH = pl.DeviceIdType.MESH


def spill_kernel(n, hot, rows_ref, out, send, recv, own_sem):
    me = lax.axis_index("dp")
    r = lax.axis_index("row")
    barrier = pltpu.get_barrier_semaphore()

    def copy(j):
        to = (hot + j) % n
        return pltpu.make_async_remote_copy(
            src_ref=rows_ref.at[to],
            dst_ref=out,
            send_sem=send.at[j - 1],
            recv_sem=recv,
            device_id=(to, r),
            device_id_type=MESH,
        )

    @pl.when(me == hot)
    def _():
        for j in range(1, n):
            pl.semaphore_signal(
                barrier, inc=1, device_id=((hot + j) % n, r), device_id_type=MESH
            )

    @pl.when(me != hot)
    def _():
        pl.semaphore_signal(barrier, inc=1, device_id=(hot, r), device_id_type=MESH)

    pl.semaphore_wait(barrier, 1 + (me == hot).astype(jnp.int32) * (n - 2))

    @pl.when(me == hot)
    def _():
        for j in range(1, n):
            copy(j).start()
        own = pltpu.make_async_copy(rows_ref.at[hot], out, own_sem)
        own.start()
        own.wait()
        for j in range(1, n):
            copy(j).wait_send()

    @pl.when(me != hot)
    def _():
        copy(1).wait_recv()


def spill(n, hot, rows):
    vmem = pl.BlockSpec(memory_space=pltpu.VMEM)
    dma = pltpu.SemaphoreType.DMA
    return pl.pallas_call(
        functools.partial(spill_kernel, n, hot),
        name=f"spill_{hot}",
        out_shape=jax.ShapeDtypeStruct(rows.shape[1:], rows.dtype),
        in_specs=[vmem],
        out_specs=vmem,
        scratch_shapes=[dma((n - 1,)), dma(()), dma(())],
        compiler_params=pltpu.CompilerParams(collective_id=3 + hot, has_side_effects=True),
    )(rows)


def fetch_hard(cached, hard_shard, hard_row, n_data):
    row_count, hard_count = hard_shard.shape
    width_dev = cached.shape[1]
    capacity = min(row_count, 3 * row_count * hard_count // n_data)
    others = -(-(row_count * hard_count - capacity) // (n_data - 1))
    common = min(capacity - 16, -(-others // 16) * 16)
    owners = hard_shard.reshape(-1)
    wanted = hard_row.reshape(-1)
    one_hot = (owners[:, None] == jnp.arange(n_data, dtype=jnp.int32)[None, :]).astype(jnp.int32)
    before = jnp.cumsum(one_hot, axis=0) - one_hot
    slot_index = jnp.sum(before * one_hot, axis=1)
    hot = jnp.argmax(jnp.sum(one_hot, axis=0)).astype(jnp.int32)
    target = owners * capacity + slot_index
    requests = (
        jnp.zeros((n_data * capacity,), jnp.int32).at[target].set(wanted).reshape(n_data, capacity)
    )
    asked_rows = lax.all_to_all(requests, "dp", split_axis=0, concat_axis=0, tiled=True)
    picked = jnp.take(cached, asked_rows[:, :common].reshape(-1), axis=0, mode="clip")
    picked = picked.reshape(n_data, common, width_dev)
    replies = lax.all_to_all(picked, "dp", split_axis=0, concat_axis=0, tiled=True)
    extra = jnp.take(cached, asked_rows[:, common:].reshape(-1), axis=0, mode="clip")
    extra = extra.reshape(n_data, capacity - common, width_dev)
    spilled = lax.switch(hot, [functools.partial(spill, n_data, k) for k in range(n_data)], extra)
    reply_rows = jnp.concatenate([replies.reshape(n_data * common, width_dev), spilled], axis=0)
    place = jnp.where(
        slot_index < common, owners * common + slot_index, n_data * common + slot_index - common
    )
    by_slot = place.reshape(row_count, hard_count).T.reshape(-1)
    hard_rows = jnp.take(reply_rows, by_slot, axis=0, mode="clip")
    return hard_rows.reshape(hard_count, row_count, width_dev)


def gather_kernel(n, n_row, q_ref, p_ref, pall, qall, lsum, lpart, lrecv,
                  gsend, grecv, lsend, lrecv_sem, own_sem):
    me = lax.axis_index("dp")
    r = lax.axis_index("row")
    lines = n // 2
    a = me // 2
    b = me % 2
    rows = q_ref.shape[0]
    part = rows // n_row
    across = a * 2 + 1 - b

    barrier = pltpu.get_barrier_semaphore()
    pl.semaphore_signal(barrier, inc=1, device_id=(across, r), device_id_type=MESH)
    for k in range(1, n_row):
        pl.semaphore_signal(
            barrier, inc=1, device_id=(me, lax.rem(r + k, n_row)), device_id_type=MESH
        )

    @pl.when(a < lines - 1)
    def _():
        pl.semaphore_signal(barrier, inc=1, device_id=(me + 2, r), device_id_type=MESH)

    @pl.when(a > 0)
    def _():
        pl.semaphore_signal(barrier, inc=1, device_id=(me - 2, r), device_id_type=MESH)

    neighbours = (a < lines - 1).astype(jnp.int32) + (a > 0).astype(jnp.int32)
    pl.semaphore_wait(barrier, n_row + neighbours)

    alls = (pall, qall)
    own = (p_ref, q_ref)

    def copy(t, kind, blk, first=False):
        to = (across, me + 2, me - 2)[kind]
        return pltpu.make_async_remote_copy(
            src_ref=own[t] if first else alls[t].at[blk],
            dst_ref=alls[t].at[blk],
            send_sem=gsend.at[t, kind, blk],
            recv_sem=grecv.at[t, blk],
            device_id=(to, r),
            device_id_type=MESH,
        )

    def arrived(t, blk):
        copy(t, 0, blk).wait_recv()

    def start_own(t):
        @pl.when(a < lines - 1)
        def _():
            copy(t, 1, me, True).start()

        @pl.when(a > 0)
        def _():
            copy(t, 2, me, True).start()

        copy(t, 0, me, True).start()

    def multiply(blk, block):
        lpart[blk] = lax.dot_general(
            q_ref[...], block, (((1,), (1,)), ((), ())), preferred_element_type=jnp.float32
        )

    def ship(blk):
        for k in range(1, n_row):
            to = lax.rem(r + k, n_row)
            ship_copy(blk, to, k).start()

    def ship_copy(blk, to, k):
        return pltpu.make_async_remote_copy(
            src_ref=lpart.at[blk, pl.ds(pl.multiple_of(to * part, part), part), :],
            dst_ref=lrecv.at[k - 1, blk],
            send_sem=lsend.at[k - 1, blk],
            recv_sem=lrecv_sem.at[k - 1, blk],
            device_id=(me, to),
            device_id_type=MESH,
        )

    def relay(t, s):
        lo = me - 2 * (s + 1)
        hi = me + 2 * (s + 1)

        @pl.when(lo >= 0)
        def _():
            arrived(t, lo)

            @pl.when(a < lines - 1)
            def _():
                copy(t, 1, lo).start()

            copy(t, 0, lo).start()

        @pl.when(hi < n)
        def _():
            arrived(t, hi)

            @pl.when(a > 0)
            def _():
                copy(t, 2, hi).start()

            copy(t, 0, hi).start()

    def logits_of(s):
        lo = me - 2 * (s + 1)
        hi = me + 2 * (s + 1)
        flip = 1 - 2 * b

        @pl.when(lo >= 0)
        def _():
            multiply(lo, pall[lo])

        @pl.when(hi < n)
        def _():
            multiply(hi, pall[hi])

        @pl.when(lo >= 0)
        def _():
            ship(lo)
            arrived(0, lo + flip)
            multiply(lo + flip, pall[lo + flip])

        @pl.when(hi < n)
        def _():
            ship(hi)
            arrived(0, hi + flip)
            multiply(hi + flip, pall[hi + flip])

        @pl.when(lo >= 0)
        def _():
            ship(lo + flip)

        @pl.when(hi < n)
        def _():
            ship(hi + flip)

    start_own(0)
    own_p = pltpu.make_async_copy(p_ref, pall.at[me], own_sem.at[0])
    own_q = pltpu.make_async_copy(q_ref, qall.at[me], own_sem.at[1])
    own_p.start()
    own_q.start()
    multiply(me, p_ref[...])
    for s in range(lines - 1):
        relay(0, s)
        if s == lines - 2:
            start_own(1)
        if s == 0:
            ship(me)
            arrived(0, across)
            multiply(across, pall[across])
            ship(across)
        else:
            logits_of(s - 1)
    for s in range(lines - 1):
        relay(1, s)
        if s == 0:
            logits_of(lines - 2)
    arrived(1, across)
    flip = 1 - 2 * b
    for s in range(lines - 1):
        lo = me - 2 * (s + 1)
        hi = me + 2 * (s + 1)

        @pl.when(lo >= 0)
        def _():
            arrived(1, lo + flip)

        @pl.when(hi < n)
        def _():
            arrived(1, hi + flip)

    base = pl.multiple_of(r * part, part)
    columns = p_ref.shape[0]
    for blk in range(n):
        total = lpart[blk, pl.ds(base, part), :]
        for k in range(1, n_row):
            ship_copy(blk, lax.rem(r + k, n_row), k).wait_recv()
            total = total + lrecv[k - 1, blk]
        lsum[:, blk * columns:(blk + 1) * columns] = total

    own_p.wait()
    own_q.wait()
    for blk in range(n):
        for k in range(1, n_row):
            ship_copy(blk, lax.rem(r + k, n_row), k).wait_send()
    for t in range(2):
        copy(t, 0, me, True).wait_send()

        @pl.when(a < lines - 1)
        def _():
            copy(t, 1, me, True).wait_send()

        @pl.when(a > 0)
        def _():
            copy(t, 2, me, True).wait_send()

        for s in range(lines - 1):
            lo = me - 2 * (s + 1)
            hi = me + 2 * (s + 1)

            @pl.when(lo >= 0)
            def _():
                copy(t, 0, lo).wait_send()

                @pl.when(a < lines - 1)
                def _():
                    copy(t, 1, lo).wait_send()

            @pl.when(hi < n)
            def _():
                copy(t, 0, hi).wait_send()

                @pl.when(a > 0)
                def _():
                    copy(t, 2, hi).wait_send()


def gather_and_logits(queries, passages, n, n_row):
    rows, width = queries.shape
    prows = passages.shape[0]
    part = rows // n_row
    vmem = pl.BlockSpec(memory_space=pltpu.VMEM)
    return pl.pallas_call(
        functools.partial(gather_kernel, n, n_row),
        name="gather_logits",
        out_shape=(
            jax.ShapeDtypeStruct((n, prows, width), passages.dtype),
            jax.ShapeDtypeStruct((n, rows, width), queries.dtype),
            jax.ShapeDtypeStruct((part, n * prows), jnp.float32),
        ),
        in_specs=[vmem, vmem],
        out_specs=(vmem, vmem, vmem),
        scratch_shapes=[
            pltpu.VMEM((n, rows, prows), jnp.float32),
            pltpu.VMEM((n_row - 1, n, part, prows), jnp.float32),
            pltpu.SemaphoreType.DMA((2, 3, n)),
            pltpu.SemaphoreType.DMA((2, n)),
            pltpu.SemaphoreType.DMA((n_row - 1, n)),
            pltpu.SemaphoreType.DMA((n_row - 1, n)),
            pltpu.SemaphoreType.DMA((2,)),
        ],
        compiler_params=pltpu.CompilerParams(
            collective_id=0, has_side_effects=True, vmem_limit_bytes=56 * 2**20
        ),
    )(queries, passages)


def weights_kernel(n, n_row, columns, w_ref, loss_ref, wrow, wcol, table, dsend, drecv, tsend,
                   trecv, rsend, rrecv, own_sem):
    me = lax.axis_index("dp")
    r = lax.axis_index("row")
    n_line = n_row // 2
    y = r // 2
    core = r % 2
    partner = y * 2 + 1 - core
    barrier = pltpu.get_barrier_semaphore()
    for j in range(1, n):
        pl.semaphore_signal(
            barrier, inc=1, device_id=(lax.rem(me + j, n), r), device_id_type=MESH
        )
    for k in range(1, n_line):
        pl.semaphore_signal(
            barrier, inc=1, device_id=(me, lax.rem(r + 2 * k, n_row)), device_id_type=MESH
        )
    pl.semaphore_signal(barrier, inc=1, device_id=(me, partner), device_id_type=MESH)
    pl.semaphore_wait(barrier, n + n_line - 1)

    def across(j):
        to = lax.rem(me + j, n)
        return pltpu.make_async_remote_copy(
            src_ref=w_ref.at[:, pl.ds(pl.multiple_of(to * columns, columns), columns)],
            dst_ref=wcol.at[y, core, me],
            send_sem=dsend.at[j - 1],
            recv_sem=drecv.at[j - 1],
            device_id=(to, r),
            device_id_type=MESH,
        )

    def tell(j):
        return pltpu.make_async_remote_copy(
            src_ref=loss_ref,
            dst_ref=table.at[y, core, me],
            send_sem=tsend.at[j - 1],
            recv_sem=trecv.at[j - 1],
            device_id=(lax.rem(me + j, n), r),
            device_id_type=MESH,
        )

    def along(which, k):
        out = (wrow, wcol, table)[which]
        return pltpu.make_async_remote_copy(
            src_ref=w_ref if which == 0 else out.at[y, core],
            dst_ref=out.at[y, core],
            send_sem=rsend.at[which, k - 1],
            recv_sem=rrecv.at[which, k - 1],
            device_id=(me, lax.rem(r + 2 * k, n_row)),
            device_id_type=MESH,
        )

    def beside(which):
        out = (wrow, wcol, table)[which]
        return pltpu.make_async_remote_copy(
            src_ref=out.at[:, core],
            dst_ref=out.at[:, core],
            send_sem=rsend.at[which, n_line - 1],
            recv_sem=rrecv.at[which, n_line - 1],
            device_id=(me, partner),
            device_id_type=MESH,
        )

    for j in range(1, n):
        across(j).start()
        tell(j).start()
    for k in range(1, n_line):
        along(0, k).start()
    owns = (
        pltpu.make_async_copy(w_ref, wrow.at[y, core], own_sem.at[0]),
        pltpu.make_async_copy(
            w_ref.at[:, pl.ds(pl.multiple_of(me * columns, columns), columns)],
            wcol.at[y, core, me],
            own_sem.at[1],
        ),
        pltpu.make_async_copy(loss_ref, table.at[y, core, me], own_sem.at[2]),
    )
    for own in owns:
        own.start()
    for own in owns:
        own.wait()
    for j in range(1, n):
        across(j).wait_recv()
        tell(j).wait_recv()
    for k in range(1, n_line):
        along(1, k).start()
        along(2, k).start()
    for which in range(3):
        for k in range(1, n_line):
            along(which, k).wait_recv()
        beside(which).start()
    for which in range(3):
        beside(which).wait_recv()
    for j in range(1, n):
        across(j).wait_send()
        tell(j).wait_send()
    for which in range(3):
        for k in range(1, n_line):
            along(which, k).wait_send()
        beside(which).wait_send()


def exchange_weights(weights_ext, loss_tile, n, n_row, columns):
    part, wide = weights_ext.shape
    vmem = pl.BlockSpec(memory_space=pltpu.VMEM)
    dma = pltpu.SemaphoreType.DMA
    n_line = n_row // 2
    return pl.pallas_call(
        functools.partial(weights_kernel, n, n_row, columns),
        name="exchange_weights",
        out_shape=(
            jax.ShapeDtypeStruct((n_line, 2, part, wide), weights_ext.dtype),
            jax.ShapeDtypeStruct((n_line, 2, n, part, columns), weights_ext.dtype),
            jax.ShapeDtypeStruct((n_line, 2, n) + loss_tile.shape, loss_tile.dtype),
        ),
        in_specs=[vmem, vmem],
        out_specs=(vmem, vmem, vmem),
        scratch_shapes=[
            dma((n - 1,)), dma((n - 1,)), dma((n - 1,)), dma((n - 1,)),
            dma((3, n_line)), dma((3, n_line)), dma((3,)),
        ],
        compiler_params=pltpu.CompilerParams(collective_id=1, has_side_effects=True),
    )(weights_ext, loss_tile)


def hard_kernel(n_row, x_ref, out, send, recv, own_sem):
    me = lax.axis_index("dp")
    r = lax.axis_index("row")
    barrier = pltpu.get_barrier_semaphore()
    for k in range(1, n_row):
        pl.semaphore_signal(
            barrier, inc=1, device_id=(me, lax.rem(r + k, n_row)), device_id_type=MESH
        )
    pl.semaphore_wait(barrier, n_row - 1)

    def along(k):
        return pltpu.make_async_remote_copy(
            src_ref=x_ref,
            dst_ref=out.at[r],
            send_sem=send.at[k - 1],
            recv_sem=recv.at[k - 1],
            device_id=(me, lax.rem(r + k, n_row)),
            device_id_type=MESH,
        )

    for k in range(1, n_row):
        along(k).start()
    own = pltpu.make_async_copy(x_ref, out.at[r], own_sem)
    own.start()
    own.wait()
    for k in range(1, n_row):
        along(k).wait()


def gather_hard(partial_hard, n_row):
    vmem = pl.BlockSpec(memory_space=pltpu.VMEM)
    dma = pltpu.SemaphoreType.DMA
    return pl.pallas_call(
        functools.partial(hard_kernel, n_row),
        name="gather_hard",
        out_shape=jax.ShapeDtypeStruct((n_row,) + partial_hard.shape, partial_hard.dtype),
        in_specs=[vmem],
        out_specs=vmem,
        scratch_shapes=[dma((n_row - 1,)), dma((n_row - 1,)), dma(())],
        compiler_params=pltpu.CompilerParams(collective_id=2, has_side_effects=True),
    )(partial_hard)


def softmax_rows(summed, summed_hard, sources, block_source, first_row, logit_scale):
    logits = logit_scale * summed
    hard_logits = logit_scale * summed_hard
    columns = jnp.arange(logits.shape[1], dtype=jnp.int32)
    targets = first_row + jnp.arange(logits.shape[0], dtype=jnp.int32)
    column_source = jnp.repeat(block_source, BLOCK)
    positive = columns[None, :] == targets[:, None]
    allowed = (sources[:, None] != column_source[None, :]) | positive
    masked = jnp.where(allowed, logits, NEG_FILL)
    maximum = jnp.maximum(jnp.max(masked, axis=1), jnp.max(hard_logits, axis=1))
    exponent = jnp.exp(masked - maximum[:, None])
    hard_expo = jnp.exp(hard_logits - maximum[:, None])
    totals = jnp.sum(exponent, axis=1) + jnp.sum(hard_expo, axis=1)
    pos_logit = jnp.sum(jnp.where(positive, logits, 0.0), axis=1)
    per_query = maximum + jnp.log(totals) - pos_logit
    weights = (exponent / totals[:, None] - positive.astype(jnp.float32)).astype(jnp.bfloat16)
    hard_weights = (hard_expo / totals[:, None]).astype(jnp.bfloat16)
    return (weights, hard_weights, jnp.sum(per_query))


def on_device(queries, passages, cached, hard_shard, hard_row, query_source, block_source):
    row_count, width = queries.shape
    columns = passages.shape[0]
    n_data = lax.axis_size("dp")
    n_row = lax.axis_size("row")
    part = row_count // n_row
    logit_scale = 1.0 / math.sqrt(D)
    hard_rows = fetch_hard(cached, hard_shard, hard_row, n_data)
    hard_count = hard_rows.shape[0]
    pall, qall, summed = gather_and_logits(queries, passages, n_data, n_row)
    partial_hard = jnp.sum(
        queries.astype(jnp.float32)[None] * hard_rows.astype(jnp.float32), axis=2
    )
    partial_hard = jnp.pad(partial_hard, ((0, -hard_count % 8), (0, 0)))
    summed_hard = jnp.sum(gather_hard(partial_hard, n_row), axis=0)[:hard_count]
    row_at = lax.axis_index("row") * part
    first_row = lax.axis_index("dp") * row_count + row_at
    my_hard = lax.dynamic_slice_in_dim(summed_hard, row_at, part, 1).T
    my_source = lax.dynamic_slice_in_dim(query_source, row_at, part, 0)
    weights, hard_weights, local_loss = softmax_rows(
        summed, my_hard, my_source, block_source, first_row, logit_scale
    )
    n_all = weights.shape[1]
    ext = jnp.concatenate(
        [weights, jnp.pad(hard_weights, ((0, 0), (0, LANES - hard_count)))], axis=1
    )
    loss_tile = jnp.full((8, LANES), local_loss, jnp.float32)
    wrow, wcol, losses = exchange_weights(ext, loss_tile, n_data, n_row, columns)
    loss_sum = jnp.sum(losses[:, :, :, 0, 0])
    mean_loss = loss_sum / (row_count * n_data)
    wrow = wrow.reshape(row_count, n_all + LANES)
    query_grad = jnp.dot(
        wrow[:, :n_all], pall.reshape(n_data * columns, width), preferred_element_type=jnp.float32
    )
    for h in range(hard_count):
        query_grad = query_grad + wrow[:, n_all + h:n_all + h + 1].astype(
            jnp.float32
        ) * hard_rows[h].astype(jnp.float32)
    passage_grad = lax.dot_general(
        wcol.reshape(n_row, n_data, part, columns),
        qall.reshape(n_data, n_row, part, width).transpose(1, 0, 2, 3),
        (((0, 1, 2), (0, 1, 2)), ((), ())),
        preferred_element_type=jnp.float32,
    )
    return (mean_loss, query_grad.astype(jnp.bfloat16), passage_grad.astype(jnp.bfloat16))


def fused_kernel(n, n_row, stages, direct, scale, sources_ref, shard_ref, row_ref, source_ref,
                 q_ref, p_ref, cache_ref, qgrad, pgrad, loss_out,
                 qall, cache, picked, chosen, note_own, notes, unit_notes, lpart, cpart, ypart,
                 peak, mass, stat_own, stat_all, wts, acc, pacc, xsend, xrecv, zsend, zrecv,
                 lsum, lrest, loss_own, loss_all, loss_mine, loss_beside,
                 gsend, grecv, nsend, nrecv, csend, crecv, ysend, yrecv, ssend, srecv,
                 wsend, wrecv, xs, xr, zs, zr, ms, mr, lsend, lrecv, own_sem, qstage, pstage, out_sem):
    me = lax.axis_index("dp")
    r = lax.axis_index("row")
    lines = n // 2
    far = lines - 1
    a = me // 2
    b = me % 2
    n_line = n_row // 2
    y = r // 2
    core = r % 2
    across = a * 2 + 1 - b
    partner = y * 2 + 1 - core
    rows, width = q_ref.shape
    columns = p_ref.shape[0]
    parts = columns // BLOCK
    part = rows // stages
    pair = 2 * part
    rest = part - direct
    slots = cache.shape[0]
    tile = min(width, 256)
    f32 = jnp.float32
    bf16 = jnp.bfloat16

    load_cache = pltpu.make_async_copy(cache_ref, cache, own_sem.at[0])
    load_cache.start()

    barrier = pltpu.get_barrier_semaphore()
    for j in range(1, n):
        pl.semaphore_signal(
            barrier, inc=1, device_id=(lax.rem(me + j, n), r), device_id_type=MESH
        )
    for k in range(1, n_line):
        pl.semaphore_signal(
            barrier, inc=1, device_id=(me, lax.rem(r + 2 * k, n_row)), device_id_type=MESH
        )
    pl.semaphore_signal(barrier, inc=1, device_id=(me, partner), device_id_type=MESH)

    own_q = [
        pltpu.make_async_copy(
            q_ref.at[pl.ds(q * part, part)], qall.at[a, q, b], own_sem.at[1 + q]
        )
        for q in range(stages)
    ]
    for copy in own_q:
        copy.start()
    source = source_ref[...].astype(f32)
    for s in range(n):
        named = jnp.where(shard_ref[...] == s, row_ref[...] + 1, 0)
        note_own[s, 0:1, :] = jnp.sum(named.astype(f32), axis=0, keepdims=True) - 1.0
        note_own[s, 1:2, :] = source
    pacc[...] = jnp.zeros_like(pacc)
    lsum[...] = jnp.zeros_like(lsum)
    stat_own[...] = jnp.zeros_like(stat_own)
    pl.semaphore_wait(barrier, n + n_line - 1)

    def remote(src, dst, send, recv, to):
        return pltpu.make_async_remote_copy(
            src_ref=src, dst_ref=dst, send_sem=send, recv_sem=recv,
            device_id=to, device_id_type=MESH,
        )

    head = pl.ds(0, direct)
    tail = pl.ds(direct, rest)

    def own_rows(q, start, size):
        return q_ref.at[pl.ds(pl.multiple_of(q * part + start, 16), size)]

    def column_copy(up, zi, q, first=False):
        at = qall.at[zi, q, b]
        return remote(
            own_rows(q, 0, part) if first else at, at, gsend.at[1 if up else 2],
            grecv.at[0, zi, q], (me + 2 if up else me - 2, r),
        )

    def head_copy(zi, q, first=False):
        at = qall.at[zi, q, b, head]
        return remote(
            own_rows(q, 0, direct) if first else at, at, gsend.at[0],
            grecv.at[1, zi, q], (across, r),
        )

    def tail_copy(q):
        return remote(
            own_rows(q, direct, rest), qall.at[a, q, b, tail], gsend.at[3],
            grecv.at[2, a, q], (across, r),
        )

    def tail_relay(up, zi, q):
        at = qall.at[zi, q, 1 - b, tail]
        return remote(
            at, at, gsend.at[4 if up else 5], grecv.at[2, zi, q],
            (me + 2 if up else me - 2, r),
        )

    def note_copy(j):
        to = lax.rem(me + j, n)
        return remote(
            note_own.at[to], notes.at[me], nsend.at[0], nrecv.at[0], (to, r)
        )

    def core_copy(zi, q):
        return remote(
            lpart.at[q, zi], cpart.at[q, zi // 2], csend.at[0], crecv.at[q, zi // 2],
            (me, partner),
        )

    def line_copy(zi, q, k):
        at = ypart.at[q, zi // 2, y]
        return remote(
            at, at, ysend.at[0], yrecv.at[q, zi // 2],
            (me, lax.rem(r + 2 * k, n_row)),
        )

    def stat_copy(j, q):
        to = lax.rem(me + j, n)
        return remote(
            stat_own.at[q], stat_all.at[q, me], ssend.at[0], srecv.at[q], (to, r)
        )

    def weight_copy(zi, q):
        at = wts.at[q, zi]
        return remote(at, at, wsend.at[0], wrecv.at[q, zi // 2], (me, partner))

    def cross_copy(zi, q):
        return remote(xsend.at[q, zi], xrecv.at[q, zi], xs.at[0], xr.at[q, zi], (across, r))

    between = lines > 2

    def chains(zi):
        if not between:
            return zi < 0
        return ((zi == 0) & (a == far - 1)) | ((zi == far) & (a == 1))

    def line_out(zi, q, chained):
        if chained:
            toward = (zi == far).astype(jnp.int32) * 2 - 1
            slot = lines + (zi == far).astype(jnp.int32)
            to = a + toward
        else:
            slot = a
            to = zi
        return remote(
            zsend.at[q, zi], zrecv.at[q, slot], zs.at[0], zr.at[q, slot], (to * 2 + b, r)
        )

    def line_in(zi, q):
        return remote(
            zsend.at[q, zi], zrecv.at[q, zi], zs.at[0], zr.at[q, zi], (me, r)
        )

    def chain_in(zi, q):
        slot = lines + (zi == far).astype(jnp.int32)
        return remote(
            zsend.at[q, zi], zrecv.at[q, slot], zs.at[0], zr.at[q, slot], (me, r)
        )

    def rest_copy(q):
        return remote(zsend.at[q, a, pl.ds(part, rest)], lrest.at[q], ms.at[0], mr.at[q], (across, r))

    def loss_copy(j):
        to = lax.rem(me + j, n)
        return remote(loss_own, loss_all.at[me], lsend.at[0], lrecv.at[0], (to, r))

    loss_core = remote(loss_mine, loss_beside, lsend.at[1], lrecv.at[1], (me, partner))

    def whole(ref, send, recv):
        return remote(ref, ref, send, recv, (me, r))

    peers = pl.ds(0, n - 1)

    def group(s, body):
        if s == 0:
            body(a)
            return

        @pl.loop(0, 2)
        def _(k):
            zi = a + (2 * k - 1) * s

            @pl.when((zi >= 0) & (zi < lines))
            def _():
                body(zi)

    def owned(body):
        def f(zi):
            @pl.when(zi % 2 == core)
            def _():
                body(zi)

        return f

    lane = lax.broadcasted_iota(jnp.int32, (1, pair), 1)
    right_half = (lane >= part).astype(jnp.int32)
    sub = lax.broadcasted_iota(jnp.int32, (BLOCK, pair), 0)
    over_width = (((1,), (1,)), ((), ()))
    over_rows = (((0,), (0,)), ((), ()))

    def diagonal():
        down = lax.broadcasted_iota(jnp.int32, (pair, pair), 0)
        right = lax.broadcasted_iota(jnp.int32, (pair, pair), 1)
        return down == right

    def start_own(q):
        @pl.when(a < far)
        def _():
            column_copy(True, a, q, True).start()

        @pl.when(a > 0)
        def _():
            column_copy(False, a, q, True).start()

        tail_copy(q).start()
        head_copy(a, q, True).start()

    def turn(q):
        tail_copy(q).wait_recv()

        @pl.when(a < far)
        def _():
            tail_relay(True, a, q).start()

        @pl.when(a > 0)
        def _():
            tail_relay(False, a, q).start()

    def relay(s):
        def column(q):
            def body(zi):
                column_copy(True, zi, q).wait_recv()

                @pl.when((zi < a) & (a < far))
                def _():
                    column_copy(True, zi, q).start()

                @pl.when((zi > a) & (a > 0))
                def _():
                    column_copy(False, zi, q).start()

                head_copy(zi, q).start()

            return body

        def tails(q):
            def body(zi):
                tail_relay(True, zi, q).wait_recv()

                @pl.when((zi < a) & (a < far))
                def _():
                    tail_relay(True, zi, q).start()

                @pl.when((zi > a) & (a > 0))
                def _():
                    tail_relay(False, zi, q).start()

            return body

        def run(q):
            group(s, column(q))
            group(s, tails(q))

        return run

    def pick(s):
        def run(q):
            @pl.when(q % 2 == 0)
            def _():
                def body(zi):
                    named = jnp.concatenate(
                        [unit_notes[zi, q, 0:1, :], unit_notes[zi, q + 1, 0:1, :]], axis=1
                    )
                    down = lax.broadcasted_iota(jnp.int32, (2 * pair, 2 * pair), 0)
                    right = lax.broadcasted_iota(jnp.int32, (2 * pair, 2 * pair), 1)
                    named = jnp.sum(
                        jnp.where(down == right, named, 0.0), axis=1, keepdims=True
                    )
                    number = lax.broadcasted_iota(jnp.int32, (2 * pair, slots), 1).astype(f32)
                    chosen[...] = jnp.where(number == named, 1.0, 0.0).astype(bf16)
                    for t in range(0, width, tile):
                        found = jnp.dot(
                            chosen[...], cache[:, t:t + tile], preferred_element_type=f32
                        ).astype(bf16)
                        picked[zi, q, :, t:t + tile] = found[:pair]
                        picked[zi, q + 1, :, t:t + tile] = found[pair:]

                group(s, body)

        return run

    def multiply(s):
        def run(q):
            def body(zi):
                head_copy(zi, q).wait_recv()
                queries = qall[zi, q].reshape(pair, width)
                lpart[q, zi, 0:columns, :] = lax.dot_general(
                    p_ref[...], queries, over_width, preferred_element_type=f32
                )
                mixed = lax.dot_general(
                    picked[zi, q], queries, over_width, preferred_element_type=f32
                )
                hard = jnp.sum(jnp.where(diagonal(), mixed, 0.0), axis=0, keepdims=True)
                lpart[q, zi, columns:columns + 8, :] = jnp.broadcast_to(hard, (8, pair))

                @pl.when(zi % 2 != core)
                def _():
                    core_copy(zi, q).start()

            group(s, body)

        return run

    def add_core(s):
        def run(q):
            def body(zi):
                core_copy(zi, q).wait_recv()
                ypart[q, zi // 2, y] = lpart[q, zi] + cpart[q, zi // 2]
                for k in range(1, n_line):
                    line_copy(zi, q, k).start()

            group(s, owned(body))

        return run

    def scored(zi, q, t):
        values = scale * lpart[q, zi, t * BLOCK:(t + 1) * BLOCK, :]
        block = sources_ref[me * parts + t].astype(f32)
        query = (zi * 2 + right_half) * rows + q * part + lane - right_half * part
        positive = (sub + (me * columns + t * BLOCK)) == query
        allowed = (unit_notes[zi, q, 1:2, :] != block) | positive
        return jnp.where(allowed, values, NEG_FILL), positive

    def scored_hard(zi, q):
        values = scale * lpart[q, zi, columns:columns + 1, :]
        return jnp.where(unit_notes[zi, q, 0:1, :] >= 0.0, values, NEG_FILL)

    def local_stats(s):
        def run(q):
            def body(zi):
                if n_line > 1:
                    at = ypart.at[q, zi // 2, pl.ds(0, n_line - 1)]
                    whole(at, ysend.at[0], yrecv.at[q, zi // 2]).wait_recv()
                total = ypart[q, zi // 2, 0]
                for k in range(1, n_line):
                    total = total + ypart[q, zi // 2, k]
                lpart[q, zi] = total
                hard = scored_hard(zi, q)
                blocks = [scored(zi, q, t)[0] for t in range(parts)]
                top = hard
                for block in blocks:
                    top = jnp.maximum(top, jnp.max(block, axis=0, keepdims=True))
                added = jnp.exp(hard - top)
                for block in blocks:
                    added = added + jnp.sum(jnp.exp(block - top), axis=0, keepdims=True)
                stat_own[q, 0, pl.ds(zi // 2, 1), :] = top
                stat_own[q, 1, pl.ds(zi // 2, 1), :] = added

            group(s, owned(body))
            if s == far:
                for j in range(1, n):
                    stat_copy(j, q).start()
                stat_all[q, me] = stat_own[q]

        return run

    def weigh(q):
        whole(stat_all.at[q, peers], ssend.at[0], srecv.at[q]).wait_recv()
        top = stat_all[q, 0, 0]
        for j in range(1, n):
            top = jnp.maximum(top, stat_all[q, j, 0])
        total = stat_all[q, 0, 1] * jnp.exp(stat_all[q, 0, 0] - top)
        for j in range(1, n):
            total = total + stat_all[q, j, 1] * jnp.exp(stat_all[q, j, 0] - top)
        peak[...] = top
        mass[...] = total

        def body(zi):
            high = peak[pl.ds(zi // 2, 1), :]
            whole = mass[pl.ds(zi // 2, 1), :]
            own_logit = jnp.zeros((1, pair), f32)
            for t in range(parts):
                masked, positive = scored(zi, q, t)
                weight = jnp.exp(masked - high) / whole - positive.astype(f32)
                wts[q, zi, t * BLOCK:(t + 1) * BLOCK, :] = weight.astype(bf16)
                own_logit = own_logit + jnp.sum(
                    jnp.where(positive, masked, 0.0), axis=0, keepdims=True
                )
            hard = jnp.exp(scored_hard(zi, q) - high) / whole
            wts[q, zi, columns:columns + 16, :] = jnp.broadcast_to(hard, (16, pair)).astype(bf16)
            weight_copy(zi, q).start()
            counted = ((zi * 2 + right_half) == me).astype(jnp.int32) > 0
            lsum[...] += jnp.where(counted, high + jnp.log(whole) - own_logit, 0.0)

        @pl.loop(0, lines)
        def _(zi):
            owned(body)(zi)

    def send_across(q):
        def body(zi):
            @pl.when(zi % 2 != core)
            def _():
                weight_copy(zi, q).wait_recv()

            hard = wts[q, zi, columns:columns + 1, :].astype(f32)
            chooser = jnp.where(diagonal(), hard, 0.0).astype(bf16)
            for t in range(0, width, tile):
                out = lax.dot_general(
                    wts[q, zi, 0:columns, :], p_ref[:, t:t + tile], over_rows,
                    preferred_element_type=f32,
                )
                acc[q, zi, :, t:t + tile] = out + jnp.dot(
                    chooser, picked[zi, q, :, t:t + tile], preferred_element_type=f32
                )
            other = pl.ds(pl.multiple_of((1 - b) * part, part), direct)
            xsend[q, zi] = acc[q, zi, other, :].astype(bf16)
            cross_copy(zi, q).start()

        for s in range(far, -1, -1):
            group(s, body)

    mine = pl.ds(pl.multiple_of(b * part, part), part)
    mine_head = pl.ds(pl.multiple_of(b * part, part), direct)
    mine_tail = pl.ds(pl.multiple_of(b * part + direct, 16), rest)
    other_tail = pl.ds(pl.multiple_of((1 - b) * part + direct, 16), rest)

    def add_line(zi, q, slot):
        acc[q, zi, mine, :] += zrecv[q, slot, 0:part, :].astype(f32)
        acc[q, zi, other_tail, :] += zrecv[q, slot, part:part + rest, :].astype(f32)

    def pass_on(s):
        def run(q):
            def body(zi):
                cross_copy(zi, q).wait_recv()
                acc[q, zi, mine_head, :] += xrecv[q, zi].astype(f32)

                @pl.when(chains(zi))
                def _():
                    chain_in(zi, q).wait_recv()
                    add_line(zi, q, lines + (zi == far).astype(jnp.int32))

                zsend[q, zi, 0:part, :] = acc[q, zi, mine, :].astype(bf16)
                zsend[q, zi, part:part + rest, :] = acc[q, zi, other_tail, :].astype(bf16)
                line_out(zi, q, between and s == far).start()

            group(s, body)

        return run

    def gather_own(q):
        cross_copy(a, q).wait_recv()
        acc[q, a, mine_head, :] += xrecv[q, a].astype(f32)

        def body(zi):
            line_in(zi, q).wait_recv()
            add_line(a, q, zi)

        for s in range(far - 1 if between else far, 0, -1):
            group(s, body)
        zsend[q, a, part:part + rest, :] = acc[q, a, other_tail, :].astype(bf16)
        rest_copy(q).start()

    def give_queries(q):
        at = pl.ds(pl.multiple_of(q * part, part), part)
        return pltpu.make_async_copy(qstage.at[at], qgrad.at[at], out_sem.at[q])

    give_passages = pltpu.make_async_copy(pstage, pgrad, out_sem.at[stages])

    def finish(q):
        rest_copy(q).wait_recv()
        acc[q, a, mine_tail, :] += lrest[q].astype(f32)
        qstage[pl.ds(pl.multiple_of(q * part, part), part), :] = acc[q, a, mine, :].astype(bf16)
        give_queries(q).start()

    def passage_terms(q):
        for t in range(0, width, tile):
            total = pacc[:, t:t + tile]
            for zi in range(lines):
                total = total + jnp.dot(
                    wts[q, zi, 0:columns, :],
                    qall[zi, q, :, :, t:t + tile].reshape(pair, tile),
                    preferred_element_type=f32,
                )
            pacc[:, t:t + tile] = total

        @pl.when(q == stages - 1)
        def _():
            pstage[...] = pacc[...].astype(bf16)
            give_passages.start()

    def tell_loss(q):
        @pl.when(q == stages - 1)
        def _():
            loss_own[...] = jnp.broadcast_to(lsum[...], (8, pair))
            for j in range(1, n):
                loss_copy(j).start()
            loss_all[me] = loss_own[...]

    for j in range(1, n):
        note_copy(j).start()
    start_own(0)

    def read_all(q):
        read_notes()

    def read_notes():
        notes[me] = note_own[me]
        whole(notes.at[peers], nsend.at[0], nrecv.at[0]).wait_recv()

        @pl.loop(0, lines)
        def _(zi):
            for q in range(stages):
                cut = slice(q * part, (q + 1) * part)
                unit_notes[zi, q] = jnp.concatenate(
                    [notes[zi * 2, :, cut], notes[zi * 2 + 1, :, cut]], axis=1
                )

        load_cache.wait()
        for copy in own_q:
            copy.wait()

    begins = [0, 2, 4, 6]
    weighs = [7, 9, 11, 13]
    acts = []
    acts += [([x + s + 3 for x in begins], local_stats(s)) for s in range(far, -1, -1)]
    acts += [([x + s + 2 for x in begins], add_core(s)) for s in range(far, -1, -1)]
    acts += [([x + 1 for x in begins], turn)]
    acts += [([x + s for x in begins], relay(s)) for s in range(1, lines)]
    acts += [([-1] + [x - 1 for x in begins[1:]], start_own)]
    acts += [([x + 1 + (between and s == far - 1) for x in weighs], pass_on(s)) for s in range(far, 0, -1)]
    acts += [(weighs, weigh)]
    acts += [([1], read_all)]
    acts += [([x + max(s, 1) for x in begins], pick(s)) for s in range(lines)]
    acts += [([x + s + 1 for x in begins], multiply(s)) for s in range(lines)]
    acts += [([x + 0 for x in weighs], send_across), ([x + 0 + 1 for x in weighs], tell_loss), ([x + 0 + 2 for x in weighs], passage_terms)]
    acts += [([x + 3 for x in weighs], gather_own), ([x + 4 for x in weighs], finish)]
    slots_in_all = max(max(times) for times, _ in acts) + 1

    @pl.loop(0, slots_in_all)
    def _(now):
        for times, act in acts:
            q = sum(i * (now == at).astype(jnp.int32) for i, at in enumerate(times))
            due = sum((now == at).astype(jnp.int32) for at in times)

            @pl.when(due > 0)
            def _():
                act(q)

    whole(loss_all.at[peers], lsend.at[0], lrecv.at[0]).wait_recv()
    sums = loss_all[0]
    for j in range(1, n):
        sums = sums + loss_all[j]
    loss_mine[...] = sums
    loss_core.start()
    loss_core.wait_recv()
    loss_out[...] = jnp.broadcast_to(
        jnp.sum(loss_mine[...] + loss_beside[...], axis=1, keepdims=True), (8, pair)
    )

    for at in range(lines):
        up = pl.ds(0, at + 1)
        down = pl.ds(0, lines - at)

        @pl.when((a == at) & (a < far))
        def _():
            whole(qall.at[up, :, 0], gsend.at[1], grecv.at[0, 0, 0]).wait_send()
            whole(qall.at[up, :, 0, pl.ds(0, rest)], gsend.at[4], grecv.at[0, 0, 0]).wait_send()

        @pl.when((a == at) & (a > 0))
        def _():
            whole(qall.at[down, :, 0], gsend.at[2], grecv.at[0, 0, 0]).wait_send()
            whole(qall.at[down, :, 0, pl.ds(0, rest)], gsend.at[5], grecv.at[0, 0, 0]).wait_send()

    held = cpart.shape[1]
    for ref, send, recv in (
        (xsend, gsend.at[0], xr.at[0, 0]),
        (lrest, gsend.at[3], mr.at[0]),
        (notes.at[peers], nsend.at[0], nrecv.at[0]),
        (cpart, csend.at[0], crecv.at[0, 0]),
        (stat_all.at[:, peers], ssend.at[0], srecv.at[0]),
        (wts.at[:, pl.ds(0, held)], wsend.at[0], wrecv.at[0, 0]),
        (xsend, xs.at[0], xr.at[0, 0]),
        (lrest, ms.at[0], mr.at[0]),
        (loss_all.at[peers], lsend.at[0], lrecv.at[0]),
    ):
        whole(ref, send, recv).wait_send()
    if far > 0:
        whole(zsend.at[:, pl.ds(0, far)], zs.at[0], zr.at[0, 0]).wait_send()
    if n_line > 1:
        sent = ypart.at[:, :, pl.ds(0, n_line - 1)]
        whole(sent, ysend.at[0], yrecv.at[0, 0]).wait_send()
    loss_core.wait_send()
    for q in range(stages):
        give_queries(q).wait()
    give_passages.wait()


def fused(queries, passages, cached, shard, row, source, block_source, n, n_row, scale):
    rows, width = queries.shape
    columns = passages.shape[0]
    slots = cached.shape[0]
    lines = n // 2
    n_line = n_row // 2
    pair = LANES
    part = pair // 2
    stages = rows // part
    direct = part * 3 // 4
    rest = part - direct
    held = (lines + 1) // 2
    f32 = jnp.float32
    bf16 = jnp.bfloat16
    vmem = pl.BlockSpec(memory_space=pltpu.VMEM)
    mem = pltpu.VMEM
    dma = pltpu.SemaphoreType.DMA
    return pl.pallas_call(
        functools.partial(fused_kernel, n, n_row, stages, direct, scale),
        name="fused_loss",
        out_shape=(
            jax.ShapeDtypeStruct((rows, width), bf16),
            jax.ShapeDtypeStruct((columns, width), bf16),
            jax.ShapeDtypeStruct((8, pair), f32),
        ),
        in_specs=[
            pl.BlockSpec(memory_space=pltpu.SMEM), vmem, vmem, vmem, vmem, vmem,
            pl.BlockSpec(memory_space=pl.ANY),
        ],
        out_specs=(
            pl.BlockSpec(memory_space=pl.ANY), pl.BlockSpec(memory_space=pl.ANY), vmem
        ),
        scratch_shapes=[
            mem((lines, stages, 2, part, width), bf16),
            mem((slots, width), bf16),
            mem((lines, stages, pair, width), bf16),
            mem((2 * pair, slots), bf16),
            mem((n, 2, rows), f32),
            mem((n, 2, rows), f32),
            mem((lines, stages, 2, pair), f32),
            mem((stages, lines, columns + 8, pair), f32),
            mem((stages, held, columns + 8, pair), f32),
            mem((stages, held, n_line, columns + 8, pair), f32),
            mem((held, pair), f32),
            mem((held, pair), f32),
            mem((stages, 2, held, pair), f32),
            mem((stages, n, 2, held, pair), f32),
            mem((stages, lines, columns + 16, pair), bf16),
            mem((stages, lines, pair, width), f32),
            mem((columns, width), f32),
            mem((stages, lines, direct, width), bf16),
            mem((stages, lines, direct, width), bf16),
            mem((stages, lines, part + rest, width), bf16),
            mem((stages, lines + 2, part + rest, width), bf16),
            mem((1, pair), f32),
            mem((stages, rest, width), bf16),
            mem((8, pair), f32),
            mem((n, 8, pair), f32),
            mem((8, pair), f32),
            mem((8, pair), f32),
            dma((6,)), dma((3, lines, stages)),
            dma((1,)), dma((1,)),
            dma((1,)), dma((stages, held)),
            dma((1,)), dma((stages, held)),
            dma((1,)), dma((stages,)),
            dma((1,)), dma((stages, held)),
            dma((1,)), dma((stages, lines)),
            dma((1,)), dma((stages, lines + 2)),
            dma((1,)), dma((stages,)),
            dma((2,)), dma((2,)),
            dma((1 + stages,)),
            mem((rows, width), bf16),
            mem((columns, width), bf16),
            dma((1 + stages,)),
        ],
        compiler_params=pltpu.CompilerParams(
            collective_id=0, has_side_effects=True, vmem_limit_bytes=56 * 2**20
        ),
    )(block_source, shard, row, source, queries, passages, cached)


def hand_out_kernel(share, q_ref, p_ref, loss_ref, q_out, p_out, loss_out, held, in_sem, out_sem):
    chunks = in_sem.shape[1]
    size = q_ref.shape[0] // chunks
    pairs = ((q_ref, q_out), (p_ref, p_out))

    def take(t, k):
        at = pl.ds(k * size, size)
        return pltpu.make_async_copy(pairs[t][0].at[at], held.at[t, at], in_sem.at[t, k])

    def give(t, k):
        at = pl.ds(k * size, size)
        return pltpu.make_async_copy(held.at[t, at], pairs[t][1].at[at], out_sem.at[t, k])

    for k in range(chunks):
        for t in range(2):
            take(t, k).start()
    loss_out[0, 0] = share * jnp.sum(loss_ref[0:1, 0:1])
    for k in range(chunks):
        for t in range(2):
            take(t, k).wait()
            give(t, k).start()
    for k in range(chunks):
        for t in range(2):
            give(t, k).wait()


def hand_out(query_grad, passage_grad, losses, share):
    rows, width = query_grad.shape
    vmem = pl.BlockSpec(memory_space=pltpu.VMEM)
    any_space = pl.BlockSpec(memory_space=pl.ANY)
    dma = pltpu.SemaphoreType.DMA
    chunks = 4
    return pl.pallas_call(
        functools.partial(hand_out_kernel, share),
        name="hand_out",
        out_shape=(
            jax.ShapeDtypeStruct(query_grad.shape, query_grad.dtype),
            jax.ShapeDtypeStruct(passage_grad.shape, passage_grad.dtype),
            jax.ShapeDtypeStruct((1, 1), jnp.float32),
        ),
        in_specs=[any_space, any_space, vmem],
        out_specs=(any_space, any_space, pl.BlockSpec(memory_space=pltpu.SMEM)),
        scratch_shapes=[
            pltpu.VMEM((2, rows, width), query_grad.dtype),
            dma((2, chunks)), dma((2, chunks)),
        ],
    )(query_grad, passage_grad, losses)


def on_device_fused(queries, passages, cached, hard_shard, hard_row, query_source, block_source):
    n = lax.axis_size("dp")
    n_row = lax.axis_size("row")
    rows = queries.shape[0]
    query_grad, passage_grad, losses = fused(
        queries, passages, cached, hard_shard.T, hard_row.T, query_source.reshape(1, rows),
        block_source, n, n_row, 1.0 / math.sqrt(D)
    )
    query_grad, passage_grad, loss = hand_out(
        query_grad, passage_grad, losses, 1.0 / (rows * n)
    )
    return (loss.reshape(()), query_grad, passage_grad)


def fits(n, n_row, rows, width, slots):
    blocks = 2 * (n * rows * width * 2 + (2 * n + 2) * rows * width + slots * width)
    half = rows // 2
    scores = n * (3 + n_row // 2) * (rows + 8) * half * 4
    return blocks + scores < 48 * 2**20 and n % 4 == 0


def solution(mesh):
    in_specs = (
        P("dp", "row"),
        P("dp", "row"),
        P("dp", "row"),
        P("dp", None),
        P("dp", None),
        P("dp"),
        P(),
    )
    out_specs = (P(), P("dp", "row"), P("dp", "row"))

    def body(queries, passages, cached, *rest):
        rows, width = queries.shape
        n, n_row = mesh.shape["dp"], mesh.shape["row"]
        if fits(n, n_row, rows, width, cached.shape[0]):
            return on_device_fused(queries, passages, cached, *rest)
        return on_device(queries, passages, cached, *rest)

    return jax.shard_map(
        body, mesh=mesh, in_specs=in_specs, out_specs=out_specs, check_vma=False
    )
```

```python
import functools
import math

import jax
import jax.numpy as jnp
from jax import lax
from jax.experimental import pallas as pl
from jax.experimental.pallas import tpu as pltpu
from jax.sharding import PartitionSpec as P

D = 4096
BLOCK = 128
LANES = 128
NEG_FILL = -1e30
MESH = pl.DeviceIdType.MESH


def spill_kernel(n, hot, rows_ref, out, send, recv, own_sem):
    me = lax.axis_index("dp")
    r = lax.axis_index("row")
    barrier = pltpu.get_barrier_semaphore()

    def copy(j):
        to = (hot + j) % n
        return pltpu.make_async_remote_copy(
            src_ref=rows_ref.at[to],
            dst_ref=out,
            send_sem=send.at[j - 1],
            recv_sem=recv,
            device_id=(to, r),
            device_id_type=MESH,
        )

    @pl.when(me == hot)
    def _():
        for j in range(1, n):
            pl.semaphore_signal(
                barrier, inc=1, device_id=((hot + j) % n, r), device_id_type=MESH
            )

    @pl.when(me != hot)
    def _():
        pl.semaphore_signal(barrier, inc=1, device_id=(hot, r), device_id_type=MESH)

    pl.semaphore_wait(barrier, 1 + (me == hot).astype(jnp.int32) * (n - 2))

    @pl.when(me == hot)
    def _():
        for j in range(1, n):
            copy(j).start()
        own = pltpu.make_async_copy(rows_ref.at[hot], out, own_sem)
        own.start()
        own.wait()
        for j in range(1, n):
            copy(j).wait_send()

    @pl.when(me != hot)
    def _():
        copy(1).wait_recv()


def spill(n, hot, rows):
    vmem = pl.BlockSpec(memory_space=pltpu.VMEM)
    dma = pltpu.SemaphoreType.DMA
    return pl.pallas_call(
        functools.partial(spill_kernel, n, hot),
        name=f"spill_{hot}",
        out_shape=jax.ShapeDtypeStruct(rows.shape[1:], rows.dtype),
        in_specs=[vmem],
        out_specs=vmem,
        scratch_shapes=[dma((n - 1,)), dma(()), dma(())],
        compiler_params=pltpu.CompilerParams(collective_id=3 + hot, has_side_effects=True),
    )(rows)


def fetch_hard(cached, hard_shard, hard_row, n_data):
    row_count, hard_count = hard_shard.shape
    width_dev = cached.shape[1]
    capacity = min(row_count, 3 * row_count * hard_count // n_data)
    others = -(-(row_count * hard_count - capacity) // (n_data - 1))
    common = min(capacity - 16, -(-others // 16) * 16)
    owners = hard_shard.reshape(-1)
    wanted = hard_row.reshape(-1)
    one_hot = (owners[:, None] == jnp.arange(n_data, dtype=jnp.int32)[None, :]).astype(jnp.int32)
    before = jnp.cumsum(one_hot, axis=0) - one_hot
    slot_index = jnp.sum(before * one_hot, axis=1)
    hot = jnp.argmax(jnp.sum(one_hot, axis=0)).astype(jnp.int32)
    target = owners * capacity + slot_index
    requests = (
        jnp.zeros((n_data * capacity,), jnp.int32).at[target].set(wanted).reshape(n_data, capacity)
    )
    asked_rows = lax.all_to_all(requests, "dp", split_axis=0, concat_axis=0, tiled=True)
    picked = jnp.take(cached, asked_rows[:, :common].reshape(-1), axis=0, mode="clip")
    picked = picked.reshape(n_data, common, width_dev)
    replies = lax.all_to_all(picked, "dp", split_axis=0, concat_axis=0, tiled=True)
    extra = jnp.take(cached, asked_rows[:, common:].reshape(-1), axis=0, mode="clip")
    extra = extra.reshape(n_data, capacity - common, width_dev)
    spilled = lax.switch(hot, [functools.partial(spill, n_data, k) for k in range(n_data)], extra)
    reply_rows = jnp.concatenate([replies.reshape(n_data * common, width_dev), spilled], axis=0)
    place = jnp.where(
        slot_index < common, owners * common + slot_index, n_data * common + slot_index - common
    )
    by_slot = place.reshape(row_count, hard_count).T.reshape(-1)
    hard_rows = jnp.take(reply_rows, by_slot, axis=0, mode="clip")
    return hard_rows.reshape(hard_count, row_count, width_dev)


def gather_kernel(n, n_row, q_ref, p_ref, pall, qall, lsum, lpart, lrecv,
                  gsend, grecv, lsend, lrecv_sem, own_sem):
    me = lax.axis_index("dp")
    r = lax.axis_index("row")
    lines = n // 2
    a = me // 2
    b = me % 2
    rows = q_ref.shape[0]
    part = rows // n_row
    across = a * 2 + 1 - b

    barrier = pltpu.get_barrier_semaphore()
    pl.semaphore_signal(barrier, inc=1, device_id=(across, r), device_id_type=MESH)
    for k in range(1, n_row):
        pl.semaphore_signal(
            barrier, inc=1, device_id=(me, lax.rem(r + k, n_row)), device_id_type=MESH
        )

    @pl.when(a < lines - 1)
    def _():
        pl.semaphore_signal(barrier, inc=1, device_id=(me + 2, r), device_id_type=MESH)

    @pl.when(a > 0)
    def _():
        pl.semaphore_signal(barrier, inc=1, device_id=(me - 2, r), device_id_type=MESH)

    neighbours = (a < lines - 1).astype(jnp.int32) + (a > 0).astype(jnp.int32)
    pl.semaphore_wait(barrier, n_row + neighbours)

    alls = (pall, qall)
    own = (p_ref, q_ref)

    def copy(t, kind, blk, first=False):
        to = (across, me + 2, me - 2)[kind]
        return pltpu.make_async_remote_copy(
            src_ref=own[t] if first else alls[t].at[blk],
            dst_ref=alls[t].at[blk],
            send_sem=gsend.at[t, kind, blk],
            recv_sem=grecv.at[t, blk],
            device_id=(to, r),
            device_id_type=MESH,
        )

    def arrived(t, blk):
        copy(t, 0, blk).wait_recv()

    def start_own(t):
        @pl.when(a < lines - 1)
        def _():
            copy(t, 1, me, True).start()

        @pl.when(a > 0)
        def _():
            copy(t, 2, me, True).start()

        copy(t, 0, me, True).start()

    def multiply(blk, block):
        lpart[blk] = lax.dot_general(
            q_ref[...], block, (((1,), (1,)), ((), ())), preferred_element_type=jnp.float32
        )

    def ship(blk):
        for k in range(1, n_row):
            to = lax.rem(r + k, n_row)
            ship_copy(blk, to, k).start()

    def ship_copy(blk, to, k):
        return pltpu.make_async_remote_copy(
            src_ref=lpart.at[blk, pl.ds(pl.multiple_of(to * part, part), part), :],
            dst_ref=lrecv.at[k - 1, blk],
            send_sem=lsend.at[k - 1, blk],
            recv_sem=lrecv_sem.at[k - 1, blk],
            device_id=(me, to),
            device_id_type=MESH,
        )

    def relay(t, s):
        lo = me - 2 * (s + 1)
        hi = me + 2 * (s + 1)

        @pl.when(lo >= 0)
        def _():
            arrived(t, lo)

            @pl.when(a < lines - 1)
            def _():
                copy(t, 1, lo).start()

            copy(t, 0, lo).start()

        @pl.when(hi < n)
        def _():
            arrived(t, hi)

            @pl.when(a > 0)
            def _():
                copy(t, 2, hi).start()

            copy(t, 0, hi).start()

    def logits_of(s):
        lo = me - 2 * (s + 1)
        hi = me + 2 * (s + 1)
        flip = 1 - 2 * b

        @pl.when(lo >= 0)
        def _():
            multiply(lo, pall[lo])

        @pl.when(hi < n)
        def _():
            multiply(hi, pall[hi])

        @pl.when(lo >= 0)
        def _():
            ship(lo)
            arrived(0, lo + flip)
            multiply(lo + flip, pall[lo + flip])

        @pl.when(hi < n)
        def _():
            ship(hi)
            arrived(0, hi + flip)
            multiply(hi + flip, pall[hi + flip])

        @pl.when(lo >= 0)
        def _():
            ship(lo + flip)

        @pl.when(hi < n)
        def _():
            ship(hi + flip)

    start_own(0)
    own_p = pltpu.make_async_copy(p_ref, pall.at[me], own_sem.at[0])
    own_q = pltpu.make_async_copy(q_ref, qall.at[me], own_sem.at[1])
    own_p.start()
    own_q.start()
    multiply(me, p_ref[...])
    for s in range(lines - 1):
        relay(0, s)
        if s == lines - 2:
            start_own(1)
        if s == 0:
            ship(me)
            arrived(0, across)
            multiply(across, pall[across])
            ship(across)
        else:
            logits_of(s - 1)
    for s in range(lines - 1):
        relay(1, s)
        if s == 0:
            logits_of(lines - 2)
    arrived(1, across)
    flip = 1 - 2 * b
    for s in range(lines - 1):
        lo = me - 2 * (s + 1)
        hi = me + 2 * (s + 1)

        @pl.when(lo >= 0)
        def _():
            arrived(1, lo + flip)

        @pl.when(hi < n)
        def _():
            arrived(1, hi + flip)

    base = pl.multiple_of(r * part, part)
    columns = p_ref.shape[0]
    for blk in range(n):
        total = lpart[blk, pl.ds(base, part), :]
        for k in range(1, n_row):
            ship_copy(blk, lax.rem(r + k, n_row), k).wait_recv()
            total = total + lrecv[k - 1, blk]
        lsum[:, blk * columns:(blk + 1) * columns] = total

    own_p.wait()
    own_q.wait()
    for blk in range(n):
        for k in range(1, n_row):
            ship_copy(blk, lax.rem(r + k, n_row), k).wait_send()
    for t in range(2):
        copy(t, 0, me, True).wait_send()

        @pl.when(a < lines - 1)
        def _():
            copy(t, 1, me, True).wait_send()

        @pl.when(a > 0)
        def _():
            copy(t, 2, me, True).wait_send()

        for s in range(lines - 1):
            lo = me - 2 * (s + 1)
            hi = me + 2 * (s + 1)

            @pl.when(lo >= 0)
            def _():
                copy(t, 0, lo).wait_send()

                @pl.when(a < lines - 1)
                def _():
                    copy(t, 1, lo).wait_send()

            @pl.when(hi < n)
            def _():
                copy(t, 0, hi).wait_send()

                @pl.when(a > 0)
                def _():
                    copy(t, 2, hi).wait_send()


def gather_and_logits(queries, passages, n, n_row):
    rows, width = queries.shape
    prows = passages.shape[0]
    part = rows // n_row
    vmem = pl.BlockSpec(memory_space=pltpu.VMEM)
    return pl.pallas_call(
        functools.partial(gather_kernel, n, n_row),
        name="gather_logits",
        out_shape=(
            jax.ShapeDtypeStruct((n, prows, width), passages.dtype),
            jax.ShapeDtypeStruct((n, rows, width), queries.dtype),
            jax.ShapeDtypeStruct((part, n * prows), jnp.float32),
        ),
        in_specs=[vmem, vmem],
        out_specs=(vmem, vmem, vmem),
        scratch_shapes=[
            pltpu.VMEM((n, rows, prows), jnp.float32),
            pltpu.VMEM((n_row - 1, n, part, prows), jnp.float32),
            pltpu.SemaphoreType.DMA((2, 3, n)),
            pltpu.SemaphoreType.DMA((2, n)),
            pltpu.SemaphoreType.DMA((n_row - 1, n)),
            pltpu.SemaphoreType.DMA((n_row - 1, n)),
            pltpu.SemaphoreType.DMA((2,)),
        ],
        compiler_params=pltpu.CompilerParams(
            collective_id=0, has_side_effects=True, vmem_limit_bytes=56 * 2**20
        ),
    )(queries, passages)


def weights_kernel(n, n_row, columns, w_ref, loss_ref, wrow, wcol, table, dsend, drecv, tsend,
                   trecv, rsend, rrecv, own_sem):
    me = lax.axis_index("dp")
    r = lax.axis_index("row")
    n_line = n_row // 2
    y = r // 2
    core = r % 2
    partner = y * 2 + 1 - core
    barrier = pltpu.get_barrier_semaphore()
    for j in range(1, n):
        pl.semaphore_signal(
            barrier, inc=1, device_id=(lax.rem(me + j, n), r), device_id_type=MESH
        )
    for k in range(1, n_line):
        pl.semaphore_signal(
            barrier, inc=1, device_id=(me, lax.rem(r + 2 * k, n_row)), device_id_type=MESH
        )
    pl.semaphore_signal(barrier, inc=1, device_id=(me, partner), device_id_type=MESH)
    pl.semaphore_wait(barrier, n + n_line - 1)

    def across(j):
        to = lax.rem(me + j, n)
        return pltpu.make_async_remote_copy(
            src_ref=w_ref.at[:, pl.ds(pl.multiple_of(to * columns, columns), columns)],
            dst_ref=wcol.at[y, core, me],
            send_sem=dsend.at[j - 1],
            recv_sem=drecv.at[j - 1],
            device_id=(to, r),
            device_id_type=MESH,
        )

    def tell(j):
        return pltpu.make_async_remote_copy(
            src_ref=loss_ref,
            dst_ref=table.at[y, core, me],
            send_sem=tsend.at[j - 1],
            recv_sem=trecv.at[j - 1],
            device_id=(lax.rem(me + j, n), r),
            device_id_type=MESH,
        )

    def along(which, k):
        out = (wrow, wcol, table)[which]
        return pltpu.make_async_remote_copy(
            src_ref=w_ref if which == 0 else out.at[y, core],
            dst_ref=out.at[y, core],
            send_sem=rsend.at[which, k - 1],
            recv_sem=rrecv.at[which, k - 1],
            device_id=(me, lax.rem(r + 2 * k, n_row)),
            device_id_type=MESH,
        )

    def beside(which):
        out = (wrow, wcol, table)[which]
        return pltpu.make_async_remote_copy(
            src_ref=out.at[:, core],
            dst_ref=out.at[:, core],
            send_sem=rsend.at[which, n_line - 1],
            recv_sem=rrecv.at[which, n_line - 1],
            device_id=(me, partner),
            device_id_type=MESH,
        )

    for j in range(1, n):
        across(j).start()
        tell(j).start()
    for k in range(1, n_line):
        along(0, k).start()
    owns = (
        pltpu.make_async_copy(w_ref, wrow.at[y, core], own_sem.at[0]),
        pltpu.make_async_copy(
            w_ref.at[:, pl.ds(pl.multiple_of(me * columns, columns), columns)],
            wcol.at[y, core, me],
            own_sem.at[1],
        ),
        pltpu.make_async_copy(loss_ref, table.at[y, core, me], own_sem.at[2]),
    )
    for own in owns:
        own.start()
    for own in owns:
        own.wait()
    for j in range(1, n):
        across(j).wait_recv()
        tell(j).wait_recv()
    for k in range(1, n_line):
        along(1, k).start()
        along(2, k).start()
    for which in range(3):
        for k in range(1, n_line):
            along(which, k).wait_recv()
        beside(which).start()
    for which in range(3):
        beside(which).wait_recv()
    for j in range(1, n):
        across(j).wait_send()
        tell(j).wait_send()
    for which in range(3):
        for k in range(1, n_line):
            along(which, k).wait_send()
        beside(which).wait_send()


def exchange_weights(weights_ext, loss_tile, n, n_row, columns):
    part, wide = weights_ext.shape
    vmem = pl.BlockSpec(memory_space=pltpu.VMEM)
    dma = pltpu.SemaphoreType.DMA
    n_line = n_row // 2
    return pl.pallas_call(
        functools.partial(weights_kernel, n, n_row, columns),
        name="exchange_weights",
        out_shape=(
            jax.ShapeDtypeStruct((n_line, 2, part, wide), weights_ext.dtype),
            jax.ShapeDtypeStruct((n_line, 2, n, part, columns), weights_ext.dtype),
            jax.ShapeDtypeStruct((n_line, 2, n) + loss_tile.shape, loss_tile.dtype),
        ),
        in_specs=[vmem, vmem],
        out_specs=(vmem, vmem, vmem),
        scratch_shapes=[
            dma((n - 1,)), dma((n - 1,)), dma((n - 1,)), dma((n - 1,)),
            dma((3, n_line)), dma((3, n_line)), dma((3,)),
        ],
        compiler_params=pltpu.CompilerParams(collective_id=1, has_side_effects=True),
    )(weights_ext, loss_tile)


def hard_kernel(n_row, x_ref, out, send, recv, own_sem):
    me = lax.axis_index("dp")
    r = lax.axis_index("row")
    barrier = pltpu.get_barrier_semaphore()
    for k in range(1, n_row):
        pl.semaphore_signal(
            barrier, inc=1, device_id=(me, lax.rem(r + k, n_row)), device_id_type=MESH
        )
    pl.semaphore_wait(barrier, n_row - 1)

    def along(k):
        return pltpu.make_async_remote_copy(
            src_ref=x_ref,
            dst_ref=out.at[r],
            send_sem=send.at[k - 1],
            recv_sem=recv.at[k - 1],
            device_id=(me, lax.rem(r + k, n_row)),
            device_id_type=MESH,
        )

    for k in range(1, n_row):
        along(k).start()
    own = pltpu.make_async_copy(x_ref, out.at[r], own_sem)
    own.start()
    own.wait()
    for k in range(1, n_row):
        along(k).wait()


def gather_hard(partial_hard, n_row):
    vmem = pl.BlockSpec(memory_space=pltpu.VMEM)
    dma = pltpu.SemaphoreType.DMA
    return pl.pallas_call(
        functools.partial(hard_kernel, n_row),
        name="gather_hard",
        out_shape=jax.ShapeDtypeStruct((n_row,) + partial_hard.shape, partial_hard.dtype),
        in_specs=[vmem],
        out_specs=vmem,
        scratch_shapes=[dma((n_row - 1,)), dma((n_row - 1,)), dma(())],
        compiler_params=pltpu.CompilerParams(collective_id=2, has_side_effects=True),
    )(partial_hard)


def softmax_rows(summed, summed_hard, sources, block_source, first_row, logit_scale):
    logits = logit_scale * summed
    hard_logits = logit_scale * summed_hard
    columns = jnp.arange(logits.shape[1], dtype=jnp.int32)
    targets = first_row + jnp.arange(logits.shape[0], dtype=jnp.int32)
    column_source = jnp.repeat(block_source, BLOCK)
    positive = columns[None, :] == targets[:, None]
    allowed = (sources[:, None] != column_source[None, :]) | positive
    masked = jnp.where(allowed, logits, NEG_FILL)
    maximum = jnp.maximum(jnp.max(masked, axis=1), jnp.max(hard_logits, axis=1))
    exponent = jnp.exp(masked - maximum[:, None])
    hard_expo = jnp.exp(hard_logits - maximum[:, None])
    totals = jnp.sum(exponent, axis=1) + jnp.sum(hard_expo, axis=1)
    pos_logit = jnp.sum(jnp.where(positive, logits, 0.0), axis=1)
    per_query = maximum + jnp.log(totals) - pos_logit
    weights = (exponent / totals[:, None] - positive.astype(jnp.float32)).astype(jnp.bfloat16)
    hard_weights = (hard_expo / totals[:, None]).astype(jnp.bfloat16)
    return (weights, hard_weights, jnp.sum(per_query))


def on_device(queries, passages, cached, hard_shard, hard_row, query_source, block_source):
    row_count, width = queries.shape
    columns = passages.shape[0]
    n_data = lax.axis_size("dp")
    n_row = lax.axis_size("row")
    part = row_count // n_row
    logit_scale = 1.0 / math.sqrt(D)
    hard_rows = fetch_hard(cached, hard_shard, hard_row, n_data)
    hard_count = hard_rows.shape[0]
    pall, qall, summed = gather_and_logits(queries, passages, n_data, n_row)
    partial_hard = jnp.sum(
        queries.astype(jnp.float32)[None] * hard_rows.astype(jnp.float32), axis=2
    )
    partial_hard = jnp.pad(partial_hard, ((0, -hard_count % 8), (0, 0)))
    summed_hard = jnp.sum(gather_hard(partial_hard, n_row), axis=0)[:hard_count]
    row_at = lax.axis_index("row") * part
    first_row = lax.axis_index("dp") * row_count + row_at
    my_hard = lax.dynamic_slice_in_dim(summed_hard, row_at, part, 1).T
    my_source = lax.dynamic_slice_in_dim(query_source, row_at, part, 0)
    weights, hard_weights, local_loss = softmax_rows(
        summed, my_hard, my_source, block_source, first_row, logit_scale
    )
    n_all = weights.shape[1]
    ext = jnp.concatenate(
        [weights, jnp.pad(hard_weights, ((0, 0), (0, LANES - hard_count)))], axis=1
    )
    loss_tile = jnp.full((8, LANES), local_loss, jnp.float32)
    wrow, wcol, losses = exchange_weights(ext, loss_tile, n_data, n_row, columns)
    loss_sum = jnp.sum(losses[:, :, :, 0, 0])
    mean_loss = loss_sum / (row_count * n_data)
    wrow = wrow.reshape(row_count, n_all + LANES)
    query_grad = jnp.dot(
        wrow[:, :n_all], pall.reshape(n_data * columns, width), preferred_element_type=jnp.float32
    )
    for h in range(hard_count):
        query_grad = query_grad + wrow[:, n_all + h:n_all + h + 1].astype(
            jnp.float32
        ) * hard_rows[h].astype(jnp.float32)
    passage_grad = lax.dot_general(
        wcol.reshape(n_row, n_data, part, columns),
        qall.reshape(n_data, n_row, part, width).transpose(1, 0, 2, 3),
        (((0, 1, 2), (0, 1, 2)), ((), ())),
        preferred_element_type=jnp.float32,
    )
    return (mean_loss, query_grad.astype(jnp.bfloat16), passage_grad.astype(jnp.bfloat16))


def fused_kernel(n, n_row, stages, direct, scale, sources_ref, shard_ref, row_ref, source_ref,
                 q_ref, p_ref, cache_ref, qgrad, pgrad, loss_out,
                 qall, cache, picked, chosen, note_own, notes, unit_notes, lpart, cpart, ypart,
                 peak, mass, stat_own, stat_all, wts, acc, pacc, xsend, xrecv, zsend, zrecv,
                 lsum, lrest, loss_own, loss_all, loss_mine, loss_beside,
                 gsend, grecv, nsend, nrecv, csend, crecv, ysend, yrecv, ssend, srecv,
                 wsend, wrecv, xs, xr, zs, zr, ms, mr, lsend, lrecv, own_sem, qstage, pstage, out_sem):
    me = lax.axis_index("dp")
    r = lax.axis_index("row")
    lines = n // 2
    far = lines - 1
    a = me // 2
    b = me % 2
    n_line = n_row // 2
    y = r // 2
    core = r % 2
    across = a * 2 + 1 - b
    partner = y * 2 + 1 - core
    rows, width = q_ref.shape
    columns = p_ref.shape[0]
    parts = columns // BLOCK
    part = rows // stages
    pair = 2 * part
    rest = part - direct
    slots = cache.shape[0]
    tile = min(width, 256)
    f32 = jnp.float32
    bf16 = jnp.bfloat16

    load_cache = pltpu.make_async_copy(cache_ref, cache, own_sem.at[0])
    load_cache.start()

    barrier = pltpu.get_barrier_semaphore()
    for j in range(1, n):
        pl.semaphore_signal(
            barrier, inc=1, device_id=(lax.rem(me + j, n), r), device_id_type=MESH
        )
    for k in range(1, n_line):
        pl.semaphore_signal(
            barrier, inc=1, device_id=(me, lax.rem(r + 2 * k, n_row)), device_id_type=MESH
        )
    pl.semaphore_signal(barrier, inc=1, device_id=(me, partner), device_id_type=MESH)

    own_q = [
        pltpu.make_async_copy(
            q_ref.at[pl.ds(q * part, part)], qall.at[a, q, b], own_sem.at[1 + q]
        )
        for q in range(stages)
    ]
    for copy in own_q:
        copy.start()
    source = source_ref[...].astype(f32)
    for s in range(n):
        named = jnp.where(shard_ref[...] == s, row_ref[...] + 1, 0)
        note_own[s, 0:1, :] = jnp.sum(named.astype(f32), axis=0, keepdims=True) - 1.0
        note_own[s, 1:2, :] = source
    pacc[...] = jnp.zeros_like(pacc)
    lsum[...] = jnp.zeros_like(lsum)
    stat_own[...] = jnp.zeros_like(stat_own)
    pl.semaphore_wait(barrier, n + n_line - 1)

    def remote(src, dst, send, recv, to):
        return pltpu.make_async_remote_copy(
            src_ref=src, dst_ref=dst, send_sem=send, recv_sem=recv,
            device_id=to, device_id_type=MESH,
        )

    head = pl.ds(0, direct)
    tail = pl.ds(direct, rest)

    def own_rows(q, start, size):
        return q_ref.at[pl.ds(pl.multiple_of(q * part + start, 16), size)]

    def column_copy(up, zi, q, first=False):
        at = qall.at[zi, q, b]
        return remote(
            own_rows(q, 0, part) if first else at, at, gsend.at[1 if up else 2],
            grecv.at[0, zi, q], (me + 2 if up else me - 2, r),
        )

    def head_copy(zi, q, first=False):
        at = qall.at[zi, q, b, head]
        return remote(
            own_rows(q, 0, direct) if first else at, at, gsend.at[0],
            grecv.at[1, zi, q], (across, r),
        )

    def tail_copy(q):
        return remote(
            own_rows(q, direct, rest), qall.at[a, q, b, tail], gsend.at[3],
            grecv.at[2, a, q], (across, r),
        )

    def tail_relay(up, zi, q):
        at = qall.at[zi, q, 1 - b, tail]
        return remote(
            at, at, gsend.at[4 if up else 5], grecv.at[2, zi, q],
            (me + 2 if up else me - 2, r),
        )

    def note_copy(j):
        to = lax.rem(me + j, n)
        return remote(
            note_own.at[to], notes.at[me], nsend.at[0], nrecv.at[0], (to, r)
        )

    def core_copy(zi, q):
        return remote(
            lpart.at[q, zi], cpart.at[q, zi // 2], csend.at[0], crecv.at[q, zi // 2],
            (me, partner),
        )

    def line_copy(zi, q, k):
        at = ypart.at[q, zi // 2, y]
        return remote(
            at, at, ysend.at[0], yrecv.at[q, zi // 2],
            (me, lax.rem(r + 2 * k, n_row)),
        )

    def stat_copy(j, q):
        to = lax.rem(me + j, n)
        return remote(
            stat_own.at[q], stat_all.at[q, me], ssend.at[0], srecv.at[q], (to, r)
        )

    def weight_copy(zi, q):
        at = wts.at[q, zi]
        return remote(at, at, wsend.at[0], wrecv.at[q, zi // 2], (me, partner))

    def cross_copy(zi, q):
        return remote(xsend.at[q, zi], xrecv.at[q, zi], xs.at[0], xr.at[q, zi], (across, r))

    between = lines > 2

    def chains(zi):
        if not between:
            return zi < 0
        return ((zi == 0) & (a == far - 1)) | ((zi == far) & (a == 1))

    def line_out(zi, q, chained):
        if chained:
            toward = (zi == far).astype(jnp.int32) * 2 - 1
            slot = lines + (zi == far).astype(jnp.int32)
            to = a + toward
        else:
            slot = a
            to = zi
        return remote(
            zsend.at[q, zi], zrecv.at[q, slot], zs.at[0], zr.at[q, slot], (to * 2 + b, r)
        )

    def line_in(zi, q):
        return remote(
            zsend.at[q, zi], zrecv.at[q, zi], zs.at[0], zr.at[q, zi], (me, r)
        )

    def chain_in(zi, q):
        slot = lines + (zi == far).astype(jnp.int32)
        return remote(
            zsend.at[q, zi], zrecv.at[q, slot], zs.at[0], zr.at[q, slot], (me, r)
        )

    def rest_copy(q):
        return remote(zsend.at[q, a, pl.ds(part, rest)], lrest.at[q], ms.at[0], mr.at[q], (across, r))

    def loss_copy(j):
        to = lax.rem(me + j, n)
        return remote(loss_own, loss_all.at[me], lsend.at[0], lrecv.at[0], (to, r))

    loss_core = remote(loss_mine, loss_beside, lsend.at[1], lrecv.at[1], (me, partner))

    def whole(ref, send, recv):
        return remote(ref, ref, send, recv, (me, r))

    peers = pl.ds(0, n - 1)

    def group(s, body):
        if s == 0:
            body(a)
            return

        @pl.loop(0, 2)
        def _(k):
            zi = a + (2 * k - 1) * s

            @pl.when((zi >= 0) & (zi < lines))
            def _():
                body(zi)

    def owned(body):
        def f(zi):
            @pl.when(zi % 2 == core)
            def _():
                body(zi)

        return f

    lane = lax.broadcasted_iota(jnp.int32, (1, pair), 1)
    right_half = (lane >= part).astype(jnp.int32)
    sub = lax.broadcasted_iota(jnp.int32, (BLOCK, pair), 0)
    over_width = (((1,), (1,)), ((), ()))
    over_rows = (((0,), (0,)), ((), ()))

    def diagonal():
        down = lax.broadcasted_iota(jnp.int32, (pair, pair), 0)
        right = lax.broadcasted_iota(jnp.int32, (pair, pair), 1)
        return down == right

    def start_own(q):
        @pl.when(a < far)
        def _():
            column_copy(True, a, q, True).start()

        @pl.when(a > 0)
        def _():
            column_copy(False, a, q, True).start()

        tail_copy(q).start()
        head_copy(a, q, True).start()

    def turn(q):
        tail_copy(q).wait_recv()

        @pl.when(a < far)
        def _():
            tail_relay(True, a, q).start()

        @pl.when(a > 0)
        def _():
            tail_relay(False, a, q).start()

    def relay(s):
        def column(q):
            def body(zi):
                column_copy(True, zi, q).wait_recv()

                @pl.when((zi < a) & (a < far))
                def _():
                    column_copy(True, zi, q).start()

                @pl.when((zi > a) & (a > 0))
                def _():
                    column_copy(False, zi, q).start()

                head_copy(zi, q).start()

            return body

        def tails(q):
            def body(zi):
                tail_relay(True, zi, q).wait_recv()

                @pl.when((zi < a) & (a < far))
                def _():
                    tail_relay(True, zi, q).start()

                @pl.when((zi > a) & (a > 0))
                def _():
                    tail_relay(False, zi, q).start()

            return body

        def run(q):
            group(s, column(q))
            group(s, tails(q))

        return run

    def pick(s):
        def run(q):
            @pl.when(q % 2 == 0)
            def _():
                def body(zi):
                    named = jnp.concatenate(
                        [unit_notes[zi, q, 0:1, :], unit_notes[zi, q + 1, 0:1, :]], axis=1
                    )
                    down = lax.broadcasted_iota(jnp.int32, (2 * pair, 2 * pair), 0)
                    right = lax.broadcasted_iota(jnp.int32, (2 * pair, 2 * pair), 1)
                    named = jnp.sum(
                        jnp.where(down == right, named, 0.0), axis=1, keepdims=True
                    )
                    number = lax.broadcasted_iota(jnp.int32, (2 * pair, slots), 1).astype(f32)
                    chosen[...] = jnp.where(number == named, 1.0, 0.0).astype(bf16)
                    for t in range(0, width, tile):
                        found = jnp.dot(
                            chosen[...], cache[:, t:t + tile], preferred_element_type=f32
                        ).astype(bf16)
                        picked[zi, q, :, t:t + tile] = found[:pair]
                        picked[zi, q + 1, :, t:t + tile] = found[pair:]

                group(s, body)

        return run

    def multiply(s):
        def run(q):
            def body(zi):
                head_copy(zi, q).wait_recv()
                queries = qall[zi, q].reshape(pair, width)
                lpart[q, zi, 0:columns, :] = lax.dot_general(
                    p_ref[...], queries, over_width, preferred_element_type=f32
                )
                mixed = lax.dot_general(
                    picked[zi, q], queries, over_width, preferred_element_type=f32
                )
                hard = jnp.sum(jnp.where(diagonal(), mixed, 0.0), axis=0, keepdims=True)
                lpart[q, zi, columns:columns + 8, :] = jnp.broadcast_to(hard, (8, pair))

                @pl.when(zi % 2 != core)
                def _():
                    core_copy(zi, q).start()

            group(s, body)

        return run

    def add_core(s):
        def run(q):
            def body(zi):
                core_copy(zi, q).wait_recv()
                ypart[q, zi // 2, y] = lpart[q, zi] + cpart[q, zi // 2]
                for k in range(1, n_line):
                    line_copy(zi, q, k).start()

            group(s, owned(body))

        return run

    def scored(zi, q, t):
        values = scale * lpart[q, zi, t * BLOCK:(t + 1) * BLOCK, :]
        block = sources_ref[me * parts + t].astype(f32)
        query = (zi * 2 + right_half) * rows + q * part + lane - right_half * part
        positive = (sub + (me * columns + t * BLOCK)) == query
        allowed = (unit_notes[zi, q, 1:2, :] != block) | positive
        return jnp.where(allowed, values, NEG_FILL), positive

    def scored_hard(zi, q):
        values = scale * lpart[q, zi, columns:columns + 1, :]
        return jnp.where(unit_notes[zi, q, 0:1, :] >= 0.0, values, NEG_FILL)

    def local_stats(s):
        def run(q):
            def body(zi):
                if n_line > 1:
                    at = ypart.at[q, zi // 2, pl.ds(0, n_line - 1)]
                    whole(at, ysend.at[0], yrecv.at[q, zi // 2]).wait_recv()
                total = ypart[q, zi // 2, 0]
                for k in range(1, n_line):
                    total = total + ypart[q, zi // 2, k]
                lpart[q, zi] = total
                hard = scored_hard(zi, q)
                blocks = [scored(zi, q, t)[0] for t in range(parts)]
                top = hard
                for block in blocks:
                    top = jnp.maximum(top, jnp.max(block, axis=0, keepdims=True))
                added = jnp.exp(hard - top)
                for block in blocks:
                    added = added + jnp.sum(jnp.exp(block - top), axis=0, keepdims=True)
                stat_own[q, 0, pl.ds(zi // 2, 1), :] = top
                stat_own[q, 1, pl.ds(zi // 2, 1), :] = added

            group(s, owned(body))
            if s == far:
                for j in range(1, n):
                    stat_copy(j, q).start()
                stat_all[q, me] = stat_own[q]

        return run

    def weigh(q):
        whole(stat_all.at[q, peers], ssend.at[0], srecv.at[q]).wait_recv()
        top = stat_all[q, 0, 0]
        for j in range(1, n):
            top = jnp.maximum(top, stat_all[q, j, 0])
        total = stat_all[q, 0, 1] * jnp.exp(stat_all[q, 0, 0] - top)
        for j in range(1, n):
            total = total + stat_all[q, j, 1] * jnp.exp(stat_all[q, j, 0] - top)
        peak[...] = top
        mass[...] = total

        def body(zi):
            high = peak[pl.ds(zi // 2, 1), :]
            whole = mass[pl.ds(zi // 2, 1), :]
            own_logit = jnp.zeros((1, pair), f32)
            for t in range(parts):
                masked, positive = scored(zi, q, t)
                weight = jnp.exp(masked - high) / whole - positive.astype(f32)
                wts[q, zi, t * BLOCK:(t + 1) * BLOCK, :] = weight.astype(bf16)
                own_logit = own_logit + jnp.sum(
                    jnp.where(positive, masked, 0.0), axis=0, keepdims=True
                )
            hard = jnp.exp(scored_hard(zi, q) - high) / whole
            wts[q, zi, columns:columns + 16, :] = jnp.broadcast_to(hard, (16, pair)).astype(bf16)
            weight_copy(zi, q).start()
            counted = ((zi * 2 + right_half) == me).astype(jnp.int32) > 0
            lsum[...] += jnp.where(counted, high + jnp.log(whole) - own_logit, 0.0)

        @pl.loop(0, lines)
        def _(zi):
            owned(body)(zi)

    def send_across(q):
        def body(zi):
            @pl.when(zi % 2 != core)
            def _():
                weight_copy(zi, q).wait_recv()

            hard = wts[q, zi, columns:columns + 1, :].astype(f32)
            chooser = jnp.where(diagonal(), hard, 0.0).astype(bf16)
            for t in range(0, width, tile):
                out = lax.dot_general(
                    wts[q, zi, 0:columns, :], p_ref[:, t:t + tile], over_rows,
                    preferred_element_type=f32,
                )
                acc[q, zi, :, t:t + tile] = out + jnp.dot(
                    chooser, picked[zi, q, :, t:t + tile], preferred_element_type=f32
                )
            other = pl.ds(pl.multiple_of((1 - b) * part, part), direct)
            xsend[q, zi] = acc[q, zi, other, :].astype(bf16)
            cross_copy(zi, q).start()

        for s in range(far, -1, -1):
            group(s, body)

    mine = pl.ds(pl.multiple_of(b * part, part), part)
    mine_head = pl.ds(pl.multiple_of(b * part, part), direct)
    mine_tail = pl.ds(pl.multiple_of(b * part + direct, 16), rest)
    other_tail = pl.ds(pl.multiple_of((1 - b) * part + direct, 16), rest)

    def add_line(zi, q, slot):
        acc[q, zi, mine, :] += zrecv[q, slot, 0:part, :].astype(f32)
        acc[q, zi, other_tail, :] += zrecv[q, slot, part:part + rest, :].astype(f32)

    def pass_on(s):
        def run(q):
            def body(zi):
                cross_copy(zi, q).wait_recv()
                acc[q, zi, mine_head, :] += xrecv[q, zi].astype(f32)

                @pl.when(chains(zi))
                def _():
                    chain_in(zi, q).wait_recv()
                    add_line(zi, q, lines + (zi == far).astype(jnp.int32))

                zsend[q, zi, 0:part, :] = acc[q, zi, mine, :].astype(bf16)
                zsend[q, zi, part:part + rest, :] = acc[q, zi, other_tail, :].astype(bf16)
                line_out(zi, q, between and s == far).start()

            group(s, body)

        return run

    def gather_own(q):
        cross_copy(a, q).wait_recv()
        acc[q, a, mine_head, :] += xrecv[q, a].astype(f32)

        def body(zi):
            line_in(zi, q).wait_recv()
            add_line(a, q, zi)

        for s in range(far - 1 if between else far, 0, -1):
            group(s, body)
        zsend[q, a, part:part + rest, :] = acc[q, a, other_tail, :].astype(bf16)
        rest_copy(q).start()

    def give_queries(q):
        at = pl.ds(pl.multiple_of(q * part, part), part)
        return pltpu.make_async_copy(qstage.at[at], qgrad.at[at], out_sem.at[q])

    give_passages = pltpu.make_async_copy(pstage, pgrad, out_sem.at[stages])

    def finish(q):
        rest_copy(q).wait_recv()
        acc[q, a, mine_tail, :] += lrest[q].astype(f32)
        qstage[pl.ds(pl.multiple_of(q * part, part), part), :] = acc[q, a, mine, :].astype(bf16)
        give_queries(q).start()

    def passage_terms(q):
        for t in range(0, width, tile):
            total = pacc[:, t:t + tile]
            for zi in range(lines):
                total = total + jnp.dot(
                    wts[q, zi, 0:columns, :],
                    qall[zi, q, :, :, t:t + tile].reshape(pair, tile),
                    preferred_element_type=f32,
                )
            pacc[:, t:t + tile] = total

        @pl.when(q == stages - 1)
        def _():
            pstage[...] = pacc[...].astype(bf16)
            give_passages.start()

    def tell_loss(q):
        @pl.when(q == stages - 1)
        def _():
            loss_own[...] = jnp.broadcast_to(lsum[...], (8, pair))
            for j in range(1, n):
                loss_copy(j).start()
            loss_all[me] = loss_own[...]

    for j in range(1, n):
        note_copy(j).start()
    start_own(0)

    def read_all(q):
        read_notes()

    def read_notes():
        notes[me] = note_own[me]
        whole(notes.at[peers], nsend.at[0], nrecv.at[0]).wait_recv()

        @pl.loop(0, lines)
        def _(zi):
            for q in range(stages):
                cut = slice(q * part, (q + 1) * part)
                unit_notes[zi, q] = jnp.concatenate(
                    [notes[zi * 2, :, cut], notes[zi * 2 + 1, :, cut]], axis=1
                )

        load_cache.wait()
        for copy in own_q:
            copy.wait()

    begins = [lines * q for q in range(stages)]
    weighs = [x + 2 * far + 4 for x in begins]
    falling = range(far, -1, -1)
    multiplied = [2 * s + 1 - (s == far) for s in range(lines)]
    counted = [min(x + 3, 2 * far + 2) for x in multiplied]

    def at(first, shift):
        return [x + shift for x in first]

    acts = [(at(begins, counted[s]), local_stats(s)) for s in falling if counted[s] < 2 * far + 2]
    acts += [(at(begins, multiplied[s] + 1), add_core(s)) for s in falling]
    acts += [(at(begins, 2 * s - 1), relay(s)) for s in range(far, 1, -1)]
    acts += [(at(begins, 1), turn), (at(begins, 1), relay(1))]
    acts += [([-1] + at(begins[1:], -2), start_own)]
    acts += [
        (at(weighs, 2 if s == far else 4 if s == far - 1 else 3), pass_on(s))
        for s in range(far, 0, -1)
    ]
    acts += [(weighs, weigh), ([1], read_all)]
    acts += [(at(begins, max(2 * s - (s == far), 1)), pick(s)) for s in range(lines)]
    acts += [(at(begins, multiplied[s]), multiply(s)) for s in range(lines)]
    acts += [
        (at(begins, counted[s]), local_stats(s)) for s in range(lines) if counted[s] == 2 * far + 2
    ]
    acts += [(weighs, send_across), (at(weighs, 1), tell_loss), (at(weighs, 2), passage_terms)]
    acts += [(at(weighs, 6), gather_own), (at(weighs, 8), finish)]
    slots_in_all = max(max(times) for times, _ in acts) + 1

    @pl.loop(0, slots_in_all)
    def _(now):
        for times, act in acts:
            q = sum(i * (now == at).astype(jnp.int32) for i, at in enumerate(times))
            due = sum((now == at).astype(jnp.int32) for at in times)

            @pl.when(due > 0)
            def _():
                act(q)

    whole(loss_all.at[peers], lsend.at[0], lrecv.at[0]).wait_recv()
    sums = loss_all[0]
    for j in range(1, n):
        sums = sums + loss_all[j]
    loss_mine[...] = sums
    loss_core.start()
    loss_core.wait_recv()
    both = loss_mine[0:1, :] + loss_beside[0:1, :]
    loss_out[...] = jnp.sum(both, axis=1, keepdims=True) * (1.0 / (rows * n))

    for at in range(lines):
        up = pl.ds(0, at + 1)
        down = pl.ds(0, lines - at)

        @pl.when((a == at) & (a < far))
        def _():
            whole(qall.at[up, :, 0], gsend.at[1], grecv.at[0, 0, 0]).wait_send()
            whole(qall.at[up, :, 0, pl.ds(0, rest)], gsend.at[4], grecv.at[0, 0, 0]).wait_send()

        @pl.when((a == at) & (a > 0))
        def _():
            whole(qall.at[down, :, 0], gsend.at[2], grecv.at[0, 0, 0]).wait_send()
            whole(qall.at[down, :, 0, pl.ds(0, rest)], gsend.at[5], grecv.at[0, 0, 0]).wait_send()

    held = cpart.shape[1]
    for ref, send, recv in (
        (xsend, gsend.at[0], xr.at[0, 0]),
        (lrest, gsend.at[3], mr.at[0]),
        (notes.at[peers], nsend.at[0], nrecv.at[0]),
        (cpart, csend.at[0], crecv.at[0, 0]),
        (stat_all.at[:, peers], ssend.at[0], srecv.at[0]),
        (wts.at[:, pl.ds(0, held)], wsend.at[0], wrecv.at[0, 0]),
        (xsend, xs.at[0], xr.at[0, 0]),
        (lrest, ms.at[0], mr.at[0]),
        (loss_all.at[peers], lsend.at[0], lrecv.at[0]),
    ):
        whole(ref, send, recv).wait_send()
    if far > 0:
        whole(zsend.at[:, pl.ds(0, far)], zs.at[0], zr.at[0, 0]).wait_send()
    if n_line > 1:
        sent = ypart.at[:, :, pl.ds(0, n_line - 1)]
        whole(sent, ysend.at[0], yrecv.at[0, 0]).wait_send()
    loss_core.wait_send()
    for q in range(stages):
        give_queries(q).wait()
    give_passages.wait()


def fused(queries, passages, cached, shard, row, source, block_source, n, n_row, scale):
    rows, width = queries.shape
    columns = passages.shape[0]
    slots = cached.shape[0]
    lines = n // 2
    n_line = n_row // 2
    pair = LANES
    part = pair // 2
    stages = rows // part
    direct = part * 3 // 4
    rest = part - direct
    held = (lines + 1) // 2
    f32 = jnp.float32
    bf16 = jnp.bfloat16
    vmem = pl.BlockSpec(memory_space=pltpu.VMEM)
    mem = pltpu.VMEM
    dma = pltpu.SemaphoreType.DMA
    return pl.pallas_call(
        functools.partial(fused_kernel, n, n_row, stages, direct, scale),
        name="fused_loss",
        out_shape=(
            jax.ShapeDtypeStruct((rows, width), bf16),
            jax.ShapeDtypeStruct((columns, width), bf16),
            jax.ShapeDtypeStruct((1, 1), f32),
        ),
        in_specs=[
            pl.BlockSpec(memory_space=pltpu.SMEM), vmem, vmem, vmem, vmem, vmem,
            pl.BlockSpec(memory_space=pl.ANY),
        ],
        out_specs=(
            pl.BlockSpec(memory_space=pl.ANY), pl.BlockSpec(memory_space=pl.ANY), vmem
        ),
        scratch_shapes=[
            mem((lines, stages, 2, part, width), bf16),
            mem((slots, width), bf16),
            mem((lines, stages, pair, width), bf16),
            mem((2 * pair, slots), bf16),
            mem((n, 2, rows), f32),
            mem((n, 2, rows), f32),
            mem((lines, stages, 2, pair), f32),
            mem((stages, lines, columns + 8, pair), f32),
            mem((stages, held, columns + 8, pair), f32),
            mem((stages, held, n_line, columns + 8, pair), f32),
            mem((held, pair), f32),
            mem((held, pair), f32),
            mem((stages, 2, held, pair), f32),
            mem((stages, n, 2, held, pair), f32),
            mem((stages, lines, columns + 16, pair), bf16),
            mem((stages, lines, pair, width), f32),
            mem((columns, width), f32),
            mem((stages, lines, direct, width), bf16),
            mem((stages, lines, direct, width), bf16),
            mem((stages, lines, part + rest, width), bf16),
            mem((stages, lines + 2, part + rest, width), bf16),
            mem((1, pair), f32),
            mem((stages, rest, width), bf16),
            mem((8, pair), f32),
            mem((n, 8, pair), f32),
            mem((8, pair), f32),
            mem((8, pair), f32),
            dma((6,)), dma((3, lines, stages)),
            dma((1,)), dma((1,)),
            dma((1,)), dma((stages, held)),
            dma((1,)), dma((stages, held)),
            dma((1,)), dma((stages,)),
            dma((1,)), dma((stages, held)),
            dma((1,)), dma((stages, lines)),
            dma((1,)), dma((stages, lines + 2)),
            dma((1,)), dma((stages,)),
            dma((2,)), dma((2,)),
            dma((1 + stages,)),
            mem((rows, width), bf16),
            mem((columns, width), bf16),
            dma((1 + stages,)),
        ],
        compiler_params=pltpu.CompilerParams(
            collective_id=0, has_side_effects=True, vmem_limit_bytes=56 * 2**20
        ),
    )(block_source, shard, row, source, queries, passages, cached)


def hand_out_kernel(q_ref, p_ref, loss_ref, q_out, p_out, loss_out, held, loss, in_sem, out_sem):
    chunks = in_sem.shape[1] - 1
    size = q_ref.shape[0] // chunks
    pairs = ((q_ref, q_out), (p_ref, p_out))

    def take(t, k):
        at = pl.ds(k * size, size)
        return pltpu.make_async_copy(pairs[t][0].at[at], held.at[t, at], in_sem.at[t, k])

    def give(t, k):
        at = pl.ds(k * size, size)
        return pltpu.make_async_copy(held.at[t, at], pairs[t][1].at[at], out_sem.at[t, k])

    take_loss = pltpu.make_async_copy(loss_ref, loss, in_sem.at[0, chunks])
    give_loss = pltpu.make_async_copy(loss, loss_out, out_sem.at[0, chunks])
    take_loss.start()
    for k in range(chunks):
        for t in range(2):
            take(t, k).start()
    take_loss.wait()
    give_loss.start()
    for k in range(chunks):
        for t in range(2):
            take(t, k).wait()
            give(t, k).start()
    for k in range(chunks):
        for t in range(2):
            give(t, k).wait()
    give_loss.wait()


def hand_out(query_grad, passage_grad, losses):
    rows, width = query_grad.shape
    any_space = pl.BlockSpec(memory_space=pl.ANY)
    dma = pltpu.SemaphoreType.DMA
    chunks = 4
    return pl.pallas_call(
        hand_out_kernel,
        name="hand_out",
        out_shape=(
            jax.ShapeDtypeStruct(query_grad.shape, query_grad.dtype),
            jax.ShapeDtypeStruct(passage_grad.shape, passage_grad.dtype),
            jax.ShapeDtypeStruct((1, 1), jnp.float32),
        ),
        in_specs=[any_space, any_space, any_space],
        out_specs=(any_space, any_space, any_space),
        scratch_shapes=[
            pltpu.VMEM((2, rows, width), query_grad.dtype),
            pltpu.VMEM((1, 1), jnp.float32),
            dma((2, chunks + 1)), dma((2, chunks + 1)),
        ],
    )(query_grad, passage_grad, losses)


def on_device_fused(queries, passages, cached, hard_shard, hard_row, query_source, block_source):
    n = lax.axis_size("dp")
    n_row = lax.axis_size("row")
    rows = queries.shape[0]
    query_grad, passage_grad, losses = fused(
        queries, passages, cached, hard_shard.T, hard_row.T, query_source.reshape(1, rows),
        block_source, n, n_row, 1.0 / math.sqrt(D)
    )
    query_grad, passage_grad, loss = hand_out(query_grad, passage_grad, losses)
    return (loss.reshape(()), query_grad, passage_grad)


def fits(n, n_row, rows, width, slots):
    blocks = 2 * (n * rows * width * 2 + (2 * n + 2) * rows * width + slots * width)
    half = rows // 2
    scores = n * (3 + n_row // 2) * (rows + 8) * half * 4
    return blocks + scores < 48 * 2**20 and n % 4 == 0


def solution(mesh):
    in_specs = (
        P("dp", "row"),
        P("dp", "row"),
        P("dp", "row"),
        P("dp", None),
        P("dp", None),
        P("dp"),
        P(),
    )
    out_specs = (P(), P("dp", "row"), P("dp", "row"))

    def body(queries, passages, cached, *rest):
        rows, width = queries.shape
        n, n_row = mesh.shape["dp"], mesh.shape["row"]
        if fits(n, n_row, rows, width, cached.shape[0]):
            return on_device_fused(queries, passages, cached, *rest)
        return on_device(queries, passages, cached, *rest)

    return jax.shard_map(
        body, mesh=mesh, in_specs=in_specs, out_specs=out_specs, check_vma=False
    )
```
